256 devices in a mesh: pa: 64 (over y, z, x_hi), gz: 4 (over x_lo, core).
Axes of the slice: x: 4 (x_hi: 2, x_lo: 2; x = x_hi * 2 + x_lo), y: 4, z: 8, core: 2. Of those that a mesh axis runs over, the one named last changes fastest.
Arguments:
- volume: float32 [128, 512, 256], P('gz', 'pa'), may hold values from -5.5 to 5.5
Outputs:
- dip_inline: float32 [128, 512, 256], P('gz', 'pa')
- dip_cross: float32 [128, 512, 256], P('gz', 'pa')
- coherence: float32 [128, 512, 256], P('gz', 'pa')
The draws below stay inside these ranges and needn't reach their ends.
All inputs are finite; a program needn't handle non-finite values.
Results may differ from the reference program's by a relative error of at most 0.000054.
Values sent between devices are 32-bit elements; how exact they have to be, the bound alone decides.
No kernel may reach another device: no remote copies, remote signals or barrier semaphores. Data moves between devices by JAX's collectives and lax.ppermute only.
A program may use at most 64 MiB of HBM per device.

```python
import math
import jax
import jax.numpy as jnp
from jax import lax

HALF = 24
GHALF = 6
NX = 256
NY = 512
NZ = 128


def draw_volume(key, part):
    keys = jax.random.split(key, 3)
    depth = jnp.arange(NZ).astype(jnp.float32)[:, None, None]
    cross = jnp.arange(NY).astype(jnp.float32)[None, :, None]
    inline = jnp.arange(NX).astype(jnp.float32)[None, None, :]
    params = jax.random.uniform(keys[0], (6,), jnp.float32)
    steepest = 0.3
    gain_spread = 0.7
    base_freq = 0.8 + 0.3 * params[0]
    inline_angle = 2.0 * math.pi * (1.0 + params[1]) / NX
    cross_angle = 2.0 * math.pi * (1.0 + params[2]) / NY
    horizon = steepest / inline_angle * jnp.sin(inline_angle * inline + 6.0 * params[3]) + steepest / cross_angle * jnp.sin(cross_angle * cross + 6.0 * params[4])
    cycles = base_freq / (2.0 * math.pi) * (depth - horizon) + params[5]
    turns = jnp.mod(cycles, 1.0)
    trace_gain = jnp.exp(jax.random.uniform(keys[1], (1, NY, NX), jnp.float32, -gain_spread, gain_spread))
    layered = 0.5 * trace_gain * jnp.cos(2.0 * math.pi * turns)
    noise = 1.5 * jnp.clip(jax.random.normal(keys[2], (NZ, NY, NX), jnp.float32), -2.9, 2.9)
    return (layered + noise).astype(jnp.float32)


def setup_inputs(seed: int = 0) -> dict:
    arg_keys = jax.random.split(jax.random.key(seed), 2)
    return {
        "volume": draw_volume(jax.random.fold_in(arg_keys[1], 71), 0),
    }


SIGMA_GRADIENT = 1.5
DECAY_LENGTH = 4.0
EPSILON = 1e-06

def tap_values(offsets, filter_kind):
    if filter_kind == 'average':
        centre = jnp.arange(-HALF, HALF + 1).astype(jnp.float32)
        values = jnp.exp(-jnp.abs(offsets) / DECAY_LENGTH) / jnp.sum(jnp.exp(-jnp.abs(centre) / DECAY_LENGTH))
        reach = HALF
    else:
        centre = jnp.arange(-GHALF, GHALF + 1).astype(jnp.float32)
        spread = 2.0 * SIGMA_GRADIENT * SIGMA_GRADIENT
        full_bell = jnp.exp(-centre * centre / spread)
        bell_curve = jnp.exp(-offsets * offsets / spread)
        if filter_kind == 'smooth':
            values = bell_curve / jnp.sqrt(jnp.sum(full_bell * full_bell))
        else:
            slopes = centre * full_bell
            values = offsets * bell_curve / jnp.sqrt(jnp.sum(slopes * slopes))
        reach = GHALF
    return jnp.where(jnp.abs(offsets) <= reach, values, 0.0)

def filter_along(source, weights, dimension, reach):
    length = source.shape[dimension]
    widths = [(0, 0)] * source.ndim
    widths[dimension] = (reach, reach)
    padded = jnp.pad(source, widths)
    summed = jnp.zeros_like(source)
    for offset in range(2 * reach + 1):
        summed = summed + weights[offset] * lax.slice_in_dim(padded, offset, offset + length, axis=dimension)
    return summed

def tensor_entry(left_grad, right_grad, average_taps):
    entry = left_grad * right_grad
    for dimension in range(3):
        entry = filter_along(entry, average_taps, dimension, HALF)
    return entry

def reference(volume):
    short_offsets = jnp.arange(-GHALF, GHALF + 1).astype(jnp.float32)
    long_offsets = jnp.arange(-HALF, HALF + 1).astype(jnp.float32)
    smooth_taps = tap_values(short_offsets, 'smooth')
    slope_taps = tap_values(short_offsets, 'slope')
    average_taps = tap_values(long_offsets, 'average')
    depth_smooth = filter_along(volume, smooth_taps, 0, GHALF)
    depth_slope = filter_along(volume, slope_taps, 0, GHALF)
    grad_x = filter_along(filter_along(depth_smooth, smooth_taps, 1, GHALF), slope_taps, 2, GHALF)
    grad_y = filter_along(filter_along(depth_smooth, slope_taps, 1, GHALF), smooth_taps, 2, GHALF)
    grad_z = filter_along(filter_along(depth_slope, smooth_taps, 1, GHALF), smooth_taps, 2, GHALF)
    tensor_xx = tensor_entry(grad_x, grad_x, average_taps)
    tensor_yy = tensor_entry(grad_y, grad_y, average_taps)
    tensor_zz = tensor_entry(grad_z, grad_z, average_taps)
    tensor_xy = tensor_entry(grad_x, grad_y, average_taps)
    tensor_xz = tensor_entry(grad_x, grad_z, average_taps)
    tensor_yz = tensor_entry(grad_y, grad_z, average_taps)
    dip_inline = -tensor_xz / (tensor_zz + EPSILON)
    dip_cross = -tensor_yz / (tensor_zz + EPSILON)
    trace_sum = tensor_xx + tensor_yy + tensor_zz
    minors = tensor_xx * tensor_yy + tensor_xx * tensor_zz + tensor_yy * tensor_zz - tensor_xy * tensor_xy - tensor_xz * tensor_xz - tensor_yz * tensor_yz
    coherence = 1.0 - 3.0 * minors / (trace_sum * trace_sum + EPSILON)
    return (dip_inline, dip_cross, coherence)
```

```python
import functools
import math

import jax
import jax.numpy as jnp
import numpy as np
from jax import lax
from jax.experimental import pallas as pl
from jax.experimental.pallas import tpu as pltpu
from jax.sharding import PartitionSpec as P

HALF = 24
GHALF = 6
SIGMA_GRADIENT = 1.5
DECAY_LENGTH = 4.0
EPSILON = 1e-06

REACH = HALF + GHALF
DECAY = math.exp(-1.0 / DECAY_LENGTH)
CUT = math.exp(-(HALF + 1) / DECAY_LENGTH)
BF16 = jnp.bfloat16
F32 = jnp.float32


def gradient_taps():
    k = np.arange(-GHALF, GHALF + 1).astype(np.float64)
    bell = np.exp(-k * k / (2.0 * SIGMA_GRADIENT**2))
    smooth = bell / np.sqrt(np.sum(bell * bell))
    slope = k * bell / np.sqrt(np.sum((k * bell) ** 2))
    return smooth, slope


def average_scale():
    k = np.arange(-HALF, HALF + 1).astype(np.float64)
    return 1.0 / np.sum(np.exp(-np.abs(k) / DECAY_LENGTH))


SMOOTH, SLOPE = gradient_taps()


def split_constant(matrix):
    matrix = matrix.astype(np.float32)
    high = matrix.astype(BF16)
    low = (matrix - high.astype(np.float32)).astype(BF16)
    return high, low


def inline_matrix(taps, length):
    reach = (len(taps) - 1) // 2
    offset = np.arange(length)[:, None] - np.arange(length)[None, :]
    inside = np.abs(offset) <= reach
    return np.where(inside, taps[np.clip(offset + reach, 0, 2 * reach)], 0.0)


def average_matrix(length):
    offset = np.abs(np.arange(length)[:, None] - np.arange(length)[None, :])
    values = np.exp(-offset / DECAY_LENGTH) * average_scale() ** 3
    return np.where(offset <= HALF, values, 0.0)


def depth_matrix(planes, halo):
    position = np.concatenate(
        [np.arange(planes), np.arange(-halo, 0), np.arange(planes, planes + halo)]
    )
    offset = position[None, :] - np.arange(planes)[:, None]
    inside = np.abs(offset) <= GHALF
    index = np.clip(offset + GHALF, 0, 2 * GHALF)
    return np.concatenate(
        [np.where(inside, SMOOTH[index], 0.0), np.where(inside, SLOPE[index], 0.0)], axis=0
    )


def split(x):
    high = x.astype(BF16)
    low = (x - high.astype(F32)).astype(BF16)
    return high, low


def dot(a, b):
    return jnp.dot(a, b, preferred_element_type=F32)


def dot3(x, w_high, w_low):
    high, low = split(x)
    return dot(high, w_high) + (dot(high, w_low) + dot(low, w_high))


def symmetric_pair(load, centre, reach, smooth, slope):
    mid = load(centre)
    total = None if smooth is None else smooth[reach] * mid
    tilt = None
    for k in range(1, reach + 1):
        after, before = load(centre + k), load(centre - k)
        if smooth is not None:
            total = total + smooth[reach + k] * (after + before)
        if slope is not None:
            term = slope[reach + k] * (after - before)
            tilt = term if tilt is None else tilt + term
    return total, tilt


def tensor_kernel(
    rows, total_rows, planes, width, halo,
    where_ref, own, other, above, below, far, near_far, up, down,
    wz_stack, wd_high, wd_low, wg_high, wg_low, ws_high, ws_low,
    out, out_last, out_first,
    zg, zd, gx, gy, gz, pre, part, ty,
):
    device = where_ref[0]
    odd = lax.rem(device, 2)
    toward = (1 - 2 * odd) * rows
    outer = rows + 2 * HALF
    smooth = [float(v) for v in SMOOTH]
    slope = [float(v) for v in SLOPE]
    trim = 4 * rows - REACH
    pieces = [
        (own, 0, rows, 0, REACH),
        (other, 0, rows, rows, REACH + toward),
        (above, 0, rows, 2 * rows, REACH - 2 * rows),
        (above, rows, rows, 3 * rows, REACH - 2 * rows + toward),
        (below, 0, rows, 4 * rows, REACH + 2 * rows),
        (below, rows, rows, 5 * rows, REACH + 2 * rows + toward),
        (far, 0, rows - trim, 6 * rows, odd * (REACH + 4 * rows)),
        (far, rows - trim, rows, 7 * rows - trim,
         (1 - odd) * (REACH - 3 * rows) + odd * (REACH + 3 * rows)),
        (near_far, 0, rows - trim, 8 * rows - trim, (1 - odd) * (REACH + 4 * rows)),
    ]
    for ref, first, count, place, base in pieces:

        def depth_row(i, carry, ref=ref, first=first, place=place, base=base):
            x = jnp.concatenate([ref[first + i], up[place + i], down[place + i]], axis=0)
            high, low = split(x)
            stacked = dot(wz_stack[...], high)
            result = stacked[: 2 * planes] + (
                stacked[2 * planes :] + dot(wz_stack[0 : 2 * planes, :], low)
            )
            zg[base + i] = result[:planes]
            zd[base + i] = result[planes:]
            return carry

        lax.fori_loop(0, count, depth_row, 0, unroll=2)

    group = 8
    for start in range(0, outer, group):

        def cross_row(r, carry, start=start):
            centre = start + r + GHALF
            position = device * rows + (start + r - HALF)
            inside = jnp.logical_and(position >= 0, position < total_rows).astype(F32)
            for z in range(0, planes, 8):
                both = symmetric_pair(
                    lambda j, z=z: zg[j, z : z + 8, :], centre, GHALF, smooth, slope
                )
                third, _ = symmetric_pair(
                    lambda j, z=z: zd[j, z : z + 8, :], centre, GHALF, smooth, None
                )
                at = pl.multiple_of(r * planes + z, 8)
                pre[0, pl.ds(at, 8), :] = both[0] * inside
                pre[1, pl.ds(at, 8), :] = both[1] * inside
                pre[2, pl.ds(at, 8), :] = third * inside
            return carry

        lax.fori_loop(0, group, cross_row, 0)
        shape = (group, planes, width)
        gx[start : start + group] = dot3(pre[0], wd_high[...], wd_low[...]).reshape(shape)
        gy[start : start + group] = dot3(pre[1], wg_high[...], wg_low[...]).reshape(shape)
        gz[start : start + group] = dot3(pre[2], wg_high[...], wg_low[...]).reshape(shape)

    def products(j, at, lanes):
        x, y, z = (ref[j, pl.ds(at, 8), lanes] for ref in (gx, gy, gz))
        return [x * x, y * y, z * z, x * y, x * z, y * z]

    for lane in range(0, width, 128):
        lanes = slice(lane, lane + 128)

        def average_rows(t, carry, lane=lane, lanes=lanes):
            at = pl.multiple_of(t * 8, 8)
            state = products(0, at, lanes)
            for j in range(1, HALF + 1):
                state = [DECAY * s + v for s, v in zip(state, products(j, at, lanes))]
            for f in range(6):
                part[f, 0] = state[f]
            for i in range(1, rows):
                new, old = products(HALF + i, at, lanes), products(i - 1, at, lanes)
                state = [DECAY * s + (v - CUT * w) for s, v, w in zip(state, new, old)]
                for f in range(6):
                    part[f, i] = state[f]
            state = [DECAY * v for v in products(outer - 1, at, lanes)]
            for j in range(outer - 2, HALF + rows - 1, -1):
                state = [DECAY * (s + v) for s, v in zip(state, products(j, at, lanes))]
            for i in range(rows - 1, -1, -1):
                for f in range(6):
                    ty[lane // 128, f, pl.ds(t * 8 * rows + i, 8, stride=rows), :] = part[f, i] + state[f]
                if i:
                    near, far_row = products(HALF + i, at, lanes), products(2 * HALF + i, at, lanes)
                    state = [
                        DECAY * (s + v) - CUT * w for s, v, w in zip(state, near, far_row)
                    ]
            return carry

        lax.fori_loop(0, planes // 8, average_rows, 0)

    for f in range(6):
        held = jnp.concatenate([ty[h, f] for h in range(width // 128)], axis=1)
        field = dot3(held, ws_high[...], ws_low[...]).reshape(planes, rows, width)
        out[:, f] = field
        out_last[:, f] = field[planes - HALF :]
        out_first[:, f] = field[:HALF]


def attribute_kernel(planes, rows, width, own, above, below, inline, cross, coherent, part):
    for lane in range(0, width, 128):
        lanes = slice(lane, lane + 128)

        def plane(z):
            if z < 0:
                return [above[HALF + z, f, :, lanes] for f in range(6)]
            if z >= planes:
                return [below[z - planes, f, :, lanes] for f in range(6)]
            return [own[z, f, :, lanes] for f in range(6)]

        state = plane(-HALF)
        for z in range(-HALF + 1, 1):
            state = [DECAY * s + v for s, v in zip(state, plane(z))]
        for f in range(6):
            part[0, f] = state[f]
        for z in range(1, planes):
            new, old = plane(z), plane(z - HALF - 1)
            state = [DECAY * s + (v - CUT * w) for s, v, w in zip(state, new, old)]
            for f in range(6):
                part[z, f] = state[f]
        state = [DECAY * v for v in plane(planes + HALF - 1)]
        for z in range(planes + HALF - 2, planes - 1, -1):
            state = [DECAY * (s + v) for s, v in zip(state, plane(z))]
        for z in range(planes - 1, -1, -1):
            xx, yy, zz, xy, xz, yz = [part[z, f] + state[f] for f in range(6)]
            scale = -1.0 / (zz + EPSILON)
            inline[z, :, lanes] = xz * scale
            cross[z, :, lanes] = yz * scale
            trace = xx + yy + zz
            minors = xx * yy + xx * zz + yy * zz - xy * xy - xz * xz - yz * yz
            coherent[z, :, lanes] = 1.0 - 3.0 * minors / (trace * trace + EPSILON)
            if z:
                near, far_plane = plane(z), plane(z + HALF)
                state = [DECAY * (s + v) - CUT * w for s, v, w in zip(state, near, far_plane)]


def send(x, axis, target):
    devices = lax.axis_size(axis)
    pairs = [(i, target(i)) for i in range(devices) if 0 <= target(i) < devices]
    return lax.ppermute(x, axis, pairs)


def local(volume):
    planes, rows, width = volume.shape
    groups = lax.axis_size("pa")
    device = lax.axis_index("pa")
    even = lax.rem(device, 2) == 0
    trim = 4 * rows - REACH
    halo = 8
    own = volume.transpose(1, 0, 2)
    other = send(own, "pa", lambda i: i ^ 1)
    pair = jnp.concatenate([own, other], axis=0)
    above = send(pair, "pa", lambda i: i + 2)
    below = send(pair, "pa", lambda i: i - 2)
    onward = jnp.where(
        even,
        above[trim:],
        jnp.concatenate([below[: rows - trim], below[rows:]], axis=0),
    )
    back = jnp.where(even, below[: rows - trim], above[trim:rows])
    far = send(onward, "pa", lambda i: i + 2 if i % 2 == 0 else i - 2)
    near_far = send(back, "pa", lambda i: i - 2 if i % 2 == 0 else i + 2)
    held = [pair, above, below, far, near_far]
    up = send(jnp.concatenate([x[:, planes - halo :] for x in held], axis=0), "gz", lambda i: i + 1)
    down = send(jnp.concatenate([x[:, :halo] for x in held], axis=0), "gz", lambda i: i - 1)

    wz_high, wz_low = split_constant(depth_matrix(planes, halo))
    weights = [jnp.asarray(np.concatenate([wz_high, wz_low], axis=0))]
    for matrix in (
        inline_matrix(SLOPE, width), inline_matrix(SMOOTH, width), average_matrix(width)
    ):
        weights += [jnp.asarray(w) for w in split_constant(matrix)]

    outer = rows + 2 * HALF
    whole = pl.BlockSpec(memory_space=pltpu.VMEM)
    tensors, last, first = pl.pallas_call(
        functools.partial(tensor_kernel, rows, rows * groups, planes, width, halo),
        out_shape=[
            jax.ShapeDtypeStruct((planes, 6, rows, width), F32),
            jax.ShapeDtypeStruct((HALF, 6, rows, width), F32),
            jax.ShapeDtypeStruct((HALF, 6, rows, width), F32),
        ],
        in_specs=[pl.BlockSpec(memory_space=pltpu.SMEM)] + [whole] * (8 + len(weights)),
        out_specs=[whole] * 3,
        scratch_shapes=[
            pltpu.VMEM((rows + 2 * REACH, planes, width), F32),
            pltpu.VMEM((rows + 2 * REACH, planes, width), F32),
            pltpu.VMEM((outer, planes, width), F32),
            pltpu.VMEM((outer, planes, width), F32),
            pltpu.VMEM((outer, planes, width), F32),
            pltpu.VMEM((3, 8 * planes, width), F32),
            pltpu.VMEM((6, rows, 8, 128), F32),
            pltpu.VMEM((width // 128, 6, planes * rows, 128), F32),
        ],
        compiler_params=pltpu.CompilerParams(vmem_limit_bytes=40 * 2**20),
        name="tensor",
    )(device.reshape(1), own, other, above, below, far, near_far, up, down, *weights)

    from_above = send(last, "gz", lambda i: i + 1)
    from_below = send(first, "gz", lambda i: i - 1)
    shape = jax.ShapeDtypeStruct((planes, rows, width), F32)
    return tuple(
        pl.pallas_call(
            functools.partial(attribute_kernel, planes, rows, width),
            out_shape=[shape] * 3,
            in_specs=[whole] * 3,
            out_specs=[whole] * 3,
            scratch_shapes=[pltpu.VMEM((planes, 6, 8, 128), F32)],
            compiler_params=pltpu.CompilerParams(vmem_limit_bytes=32 * 2**20),
            name="attributes",
        )(tensors, from_above, from_below)
    )


def solution(mesh):
    placed = P("gz", "pa", None)
    return jax.shard_map(
        local,
        mesh=mesh,
        in_specs=(placed,),
        out_specs=(placed, placed, placed),
        check_vma=False,
    )
```

```python
import functools
import math

import jax
import jax.numpy as jnp
import numpy as np
from jax import lax
from jax.experimental import pallas as pl
from jax.experimental.pallas import tpu as pltpu
from jax.sharding import PartitionSpec as P

HALF = 24
GHALF = 6
SIGMA_GRADIENT = 1.5
DECAY_LENGTH = 4.0
EPSILON = 1e-06

REACH = HALF + GHALF
DECAY = math.exp(-1.0 / DECAY_LENGTH)
CUT = math.exp(-(HALF + 1) / DECAY_LENGTH)
BF16 = jnp.bfloat16
F32 = jnp.float32


def gradient_taps():
    k = np.arange(-GHALF, GHALF + 1).astype(np.float64)
    bell = np.exp(-k * k / (2.0 * SIGMA_GRADIENT**2))
    smooth = bell / np.sqrt(np.sum(bell * bell))
    slope = k * bell / np.sqrt(np.sum((k * bell) ** 2))
    return smooth, slope


def average_scale():
    k = np.arange(-HALF, HALF + 1).astype(np.float64)
    return 1.0 / np.sum(np.exp(-np.abs(k) / DECAY_LENGTH))


SMOOTH, SLOPE = gradient_taps()


def split_constant(matrix):
    matrix = matrix.astype(np.float32)
    high = matrix.astype(BF16)
    low = (matrix - high.astype(np.float32)).astype(BF16)
    return high, low


def inline_matrix(taps, length):
    reach = (len(taps) - 1) // 2
    offset = np.arange(length)[:, None] - np.arange(length)[None, :]
    inside = np.abs(offset) <= reach
    return np.where(inside, taps[np.clip(offset + reach, 0, 2 * reach)], 0.0)


def average_matrix(length):
    offset = np.abs(np.arange(length)[:, None] - np.arange(length)[None, :])
    values = np.exp(-offset / DECAY_LENGTH) * average_scale() ** 3
    return np.where(offset <= HALF, values, 0.0)


def depth_matrix(planes, halo):
    position = np.concatenate(
        [np.arange(planes), np.arange(-halo, 0), np.arange(planes, planes + halo)]
    )
    offset = position[None, :] - np.arange(planes)[:, None]
    inside = np.abs(offset) <= GHALF
    index = np.clip(offset + GHALF, 0, 2 * GHALF)
    return np.concatenate(
        [np.where(inside, SMOOTH[index], 0.0), np.where(inside, SLOPE[index], 0.0)], axis=0
    )


def split(x):
    high = x.astype(BF16)
    low = (x - high.astype(F32)).astype(BF16)
    return high, low


def dot(a, b):
    return jnp.dot(a, b, preferred_element_type=F32)


def dot3(x, w_high, w_low):
    high, low = split(x)
    return dot(high, w_high) + (dot(high, w_low) + dot(low, w_high))


def symmetric_pair(load, centre, reach, smooth, slope):
    mid = load(centre)
    total = None if smooth is None else smooth[reach] * mid
    tilt = None
    for k in range(1, reach + 1):
        after, before = load(centre + k), load(centre - k)
        if smooth is not None:
            total = total + smooth[reach + k] * (after + before)
        if slope is not None:
            term = slope[reach + k] * (after - before)
            tilt = term if tilt is None else tilt + term
    return total, tilt


def tensor_kernel(
    rows, total_rows, tiles, width, halos, *refs
):
    where_ref, own, other, above, below, above_other, below_other, above_far, below_far, last_far = refs[:10]
    if halos:
        up, down = refs[10:12]
        refs = refs[2:]
    wz_stack, wd_high, wd_low, wg_high, wg_low, ws_high, ws_low = refs[10:17]
    outs = refs[17 : 17 + (2 if halos else 1)]
    zg, zd, gx, gy, gz, pre, part, ty = refs[-8:]
    planes = 8 * tiles
    device = where_ref[0]
    odd = lax.rem(device, 2)
    toward = (1 - 2 * odd) * rows
    outer = rows + 2 * HALF
    smooth = [float(v) for v in SMOOTH]
    slope = [float(v) for v in SLOPE]
    trim = 4 * rows - REACH
    pieces = [
        (own, 0, rows, 0, REACH),
        (other, 0, rows, rows, REACH + toward),
        (above, 0, rows, 2 * rows, REACH - 2 * rows),
        (below, 0, rows, 3 * rows, REACH + 2 * rows),
        (above_other, 0, rows, 4 * rows, REACH - 2 * rows + toward),
        (below_other, 0, rows, 5 * rows, REACH + 2 * rows + toward),
        (above_far, trim, rows - trim, 6 * rows, 0),
        (below_far, 0, rows - trim, 7 * rows - trim, REACH + 4 * rows),
        (last_far, 0, rows, 8 * rows - 2 * trim, REACH - 3 * rows * (1 - 2 * odd)),
    ]
    for ref, first, count, place, base in pieces:

        def depth_row(i, carry, ref=ref, first=first, place=place, base=base):
            x = ref[first + i]
            if halos:
                x = jnp.concatenate([x, up[place + i], down[place + i]], axis=0)
            high, low = split(x)
            stacked = dot(wz_stack[...], high)
            result = stacked[: 2 * planes] + (
                stacked[2 * planes :] + dot(wz_stack[0 : 2 * planes, :], low)
            )
            zg[base + i] = result[:planes]
            zd[base + i] = result[planes:]
            return carry

        lax.fori_loop(0, count, depth_row, 0, unroll=2)

    group = 8
    for start in range(0, outer, group):

        def cross_row(r, carry, start=start):
            centre = start + r + GHALF
            position = device * rows + (start + r - HALF)
            inside = jnp.logical_and(position >= 0, position < total_rows).astype(F32)
            for z in range(0, planes, 8):
                both = symmetric_pair(
                    lambda j, z=z: zg[j, z : z + 8, :], centre, GHALF, smooth, slope
                )
                third, _ = symmetric_pair(
                    lambda j, z=z: zd[j, z : z + 8, :], centre, GHALF, smooth, None
                )
                at = pl.multiple_of(r * planes + z, 8)
                pre[0, pl.ds(at, 8), :] = both[0] * inside
                pre[1, pl.ds(at, 8), :] = both[1] * inside
                pre[2, pl.ds(at, 8), :] = third * inside
            return carry

        lax.fori_loop(0, group, cross_row, 0)
        shape = (group, planes, width)
        gx[start : start + group] = dot3(pre[0], wd_high[...], wd_low[...]).reshape(shape)
        gy[start : start + group] = dot3(pre[1], wg_high[...], wg_low[...]).reshape(shape)
        gz[start : start + group] = dot3(pre[2], wg_high[...], wg_low[...]).reshape(shape)

    def products(j, at, lanes):
        x, y, z = (ref[j, pl.ds(at, 8), lanes] for ref in (gx, gy, gz))
        return [x * x, y * y, z * z, x * y, x * z, y * z]

    for lane in range(0, width, 128):
        lanes = slice(lane, lane + 128)

        def average_rows(t, carry, lane=lane, lanes=lanes):
            at = pl.multiple_of(t * 8, 8)
            state = products(0, at, lanes)
            for j in range(1, HALF + 1):
                state = [DECAY * s + v for s, v in zip(state, products(j, at, lanes))]
            for f in range(6):
                part[f, 0] = state[f]
            for i in range(1, rows):
                new, old = products(HALF + i, at, lanes), products(i - 1, at, lanes)
                state = [DECAY * s + (v - CUT * w) for s, v, w in zip(state, new, old)]
                for f in range(6):
                    part[f, i] = state[f]
            state = [DECAY * v for v in products(outer - 1, at, lanes)]
            for j in range(outer - 2, HALF + rows - 1, -1):
                state = [DECAY * (s + v) for s, v in zip(state, products(j, at, lanes))]
            for i in range(rows - 1, -1, -1):
                for f in range(6):
                    ty[lane // 128, f, pl.ds(t * 8 * rows + i, 8, stride=rows), :] = part[f, i] + state[f]
                if i:
                    near, far_row = products(HALF + i, at, lanes), products(2 * HALF + i, at, lanes)
                    state = [
                        DECAY * (s + v) - CUT * w for s, v, w in zip(state, near, far_row)
                    ]
            return carry

        lax.fori_loop(0, planes // 8, average_rows, 0)

    for f in range(6):
        held = jnp.concatenate([ty[h, f] for h in range(width // 128)], axis=1)
        field = dot3(held, ws_high[...], ws_low[...]).reshape(planes, rows, width)
        step = planes // len(outs)
        for n, out in enumerate(outs):
            out[:, f] = field[n * step : (n + 1) * step]


def attribute_kernel(planes, width, pieces, *refs):
    inline, cross, coherent, part = refs[-4:]
    for lane in range(0, width, 128):
        lanes = slice(lane, lane + 128)

        def plane(z):
            for ref, start in zip(refs, pieces):
                if start <= z < start + ref.shape[0]:
                    return [ref[z - start, f, :, lanes] for f in range(6)]

        state = plane(-HALF)
        for z in range(-HALF + 1, 1):
            state = [DECAY * s + v for s, v in zip(state, plane(z))]
        for f in range(6):
            part[0, f] = state[f]
        for z in range(1, planes):
            new, old = plane(z), plane(z - HALF - 1)
            state = [DECAY * s + (v - CUT * w) for s, v, w in zip(state, new, old)]
            for f in range(6):
                part[z, f] = state[f]
        state = [DECAY * v for v in plane(planes + HALF - 1)]
        for z in range(planes + HALF - 2, planes - 1, -1):
            state = [DECAY * (s + v) for s, v in zip(state, plane(z))]
        for z in range(planes - 1, -1, -1):
            xx, yy, zz, xy, xz, yz = [part[z, f] + state[f] for f in range(6)]
            scale = -1.0 / (zz + EPSILON)
            inline[z, :, lanes] = xz * scale
            cross[z, :, lanes] = yz * scale
            trace = xx + yy + zz
            minors = xx * yy + xx * zz + yy * zz - xy * xy - xz * xz - yz * yz
            coherent[z, :, lanes] = 1.0 - 3.0 * minors / (trace * trace + EPSILON)
            if z:
                near, far_plane = plane(z), plane(z + HALF)
                state = [DECAY * (s + v) - CUT * w for s, v, w in zip(state, near, far_plane)]


def send(x, axis, target):
    devices = lax.axis_size(axis)
    pairs = [(i, target(i)) for i in range(devices) if 0 <= target(i) < devices]
    return lax.ppermute(x, axis, pairs)


def local(volume):
    planes, rows, width = volume.shape
    groups = lax.axis_size("pa")
    device = lax.axis_index("pa")
    even = lax.rem(device, 2) == 0
    trim = 4 * rows - REACH
    halo = 8
    own = volume.transpose(1, 0, 2)
    above = send(own, "pa", lambda i: i + 2)
    below = send(own, "pa", lambda i: i - 2)
    other = send(own, "pa", lambda i: i ^ 1)
    above_far = send(above, "pa", lambda i: i + 2)
    below_far = send(below, "pa", lambda i: i - 2)
    above_other = send(other, "pa", lambda i: i + 2)
    below_other = send(other, "pa", lambda i: i - 2)
    last_far = send(jnp.where(even, below_far, above_far), "pa", lambda i: i ^ 1)
    pieces = [own, other, above, below, above_other, below_other, above_far, below_far, last_far]
    held = pieces[:6] + [above_far[trim:], below_far[: rows - trim], last_far]
    up = send(jnp.concatenate([x[:, planes - halo :] for x in held], axis=0), "gz", lambda i: i + 1)
    down = send(jnp.concatenate([x[:, :halo] for x in held], axis=0), "gz", lambda i: i - 1)

    weights = []
    for matrix in (
        inline_matrix(SLOPE, width), inline_matrix(SMOOTH, width), average_matrix(width)
    ):
        weights += [jnp.asarray(w) for w in split_constant(matrix)]
    matrix = depth_matrix(planes, halo)
    index = np.arange(planes)
    inner = np.logical_and(index >= halo, index < planes - halo)

    def tensors(chosen, halos, name):
        used = int(np.sum(chosen))
        columns = matrix.shape[1] if halos else planes
        part = matrix[np.concatenate([chosen, chosen])][:, :columns]
        stack = jnp.asarray(np.concatenate(split_constant(part), axis=0))
        outer = rows + 2 * HALF
        outs = 2 if halos else 1
        operands = pieces + (list(halos) if halos else []) + [stack] + weights
        return pl.pallas_call(
            functools.partial(
                tensor_kernel, rows, rows * groups, used // 8, width, bool(halos)
            ),
            out_shape=[jax.ShapeDtypeStruct((used // outs, 6, rows, width), F32)] * outs,
            in_specs=[pl.BlockSpec(memory_space=pltpu.SMEM)] + [whole] * len(operands),
            out_specs=[whole] * outs,
            scratch_shapes=[
                pltpu.VMEM((rows + 2 * REACH, used, width), F32),
                pltpu.VMEM((rows + 2 * REACH, used, width), F32),
                pltpu.VMEM((outer, used, width), F32),
                pltpu.VMEM((outer, used, width), F32),
                pltpu.VMEM((outer, used, width), F32),
                pltpu.VMEM((3, 8 * used, width), F32),
                pltpu.VMEM((6, rows, 8, 128), F32),
                pltpu.VMEM((width // 128, 6, used * rows, 128), F32),
            ],
            compiler_params=pltpu.CompilerParams(vmem_limit_bytes=28 * 2**20),
            cost_estimate=pl.CostEstimate(
                flops=8 * 10**9, bytes_accessed=4 * 2**20, transcendentals=0
            ),
            name=name,
        )(device.reshape(1), *operands)

    whole = pl.BlockSpec(memory_space=pltpu.VMEM)
    (middle,) = tensors(inner, None, "tensor_middle")
    middle_above = send(middle, "gz", lambda i: i + 1)
    middle_below = send(middle, "gz", lambda i: i - 1)
    first, last = tensors(~inner, (up, down), "tensor_ends")
    last_above = send(last, "gz", lambda i: i + 1)
    first_below = send(first, "gz", lambda i: i - 1)
    arrays = [middle_above, last_above, first, middle, last, first_below, middle_below]
    starts = [-HALF, -halo, 0, halo, planes - halo, planes, planes + halo]
    shape = jax.ShapeDtypeStruct((planes, rows, width), F32)
    return tuple(
        pl.pallas_call(
            functools.partial(attribute_kernel, planes, width, starts),
            out_shape=[shape] * 3,
            in_specs=[whole] * len(arrays),
            out_specs=[whole] * 3,
            scratch_shapes=[pltpu.VMEM((planes, 6, 8, 128), F32)],
            compiler_params=pltpu.CompilerParams(vmem_limit_bytes=28 * 2**20),
            name="attributes",
        )(*arrays)
    )


def solution(mesh):
    placed = P("gz", "pa", None)
    return jax.shard_map(
        local,
        mesh=mesh,
        in_specs=(placed,),
        out_specs=(placed, placed, placed),
        check_vma=False,
    )
```

```python
import functools
import math

import jax
import jax.numpy as jnp
import numpy as np
from jax import lax
from jax.experimental import pallas as pl
from jax.experimental.pallas import tpu as pltpu
from jax.sharding import PartitionSpec as P

HALF = 24
GHALF = 6
SIGMA_GRADIENT = 1.5
DECAY_LENGTH = 4.0
EPSILON = 1e-06

REACH = HALF + GHALF
DECAY = math.exp(-1.0 / DECAY_LENGTH)
CUT = math.exp(-(HALF + 1) / DECAY_LENGTH)
BF16 = jnp.bfloat16
F32 = jnp.float32


def gradient_taps():
    k = np.arange(-GHALF, GHALF + 1).astype(np.float64)
    bell = np.exp(-k * k / (2.0 * SIGMA_GRADIENT**2))
    smooth = bell / np.sqrt(np.sum(bell * bell))
    slope = k * bell / np.sqrt(np.sum((k * bell) ** 2))
    return smooth, slope


def average_scale():
    k = np.arange(-HALF, HALF + 1).astype(np.float64)
    return 1.0 / np.sum(np.exp(-np.abs(k) / DECAY_LENGTH))


SMOOTH, SLOPE = gradient_taps()


def split_constant(matrix):
    matrix = matrix.astype(np.float32)
    high = matrix.astype(BF16)
    low = (matrix - high.astype(np.float32)).astype(BF16)
    return high, low


def inline_matrix(taps, length):
    reach = (len(taps) - 1) // 2
    offset = np.arange(length)[:, None] - np.arange(length)[None, :]
    inside = np.abs(offset) <= reach
    return np.where(inside, taps[np.clip(offset + reach, 0, 2 * reach)], 0.0)


def average_matrix(length):
    offset = np.abs(np.arange(length)[:, None] - np.arange(length)[None, :])
    values = np.exp(-offset / DECAY_LENGTH) * average_scale() ** 3
    return np.where(offset <= HALF, values, 0.0)


def tile_matrix(rows, planes):
    def band(taps, outputs, inputs, lead):
        offset = np.arange(inputs)[None, :] - np.arange(outputs)[:, None] - lead
        inside = np.abs(offset) <= GHALF
        return np.where(inside, taps[np.clip(offset + GHALF, 0, 2 * GHALF)], 0.0)

    def pair(cross, depth):
        cross = band(cross, rows, rows + 2 * GHALF, GHALF)
        depth = band(depth, planes, 3 * planes, planes)
        return np.kron(cross, depth)

    return np.concatenate(
        [pair(SMOOTH, SMOOTH), pair(SLOPE, SMOOTH), pair(SMOOTH, SLOPE)], axis=0
    )


def split(x):
    high = x.astype(BF16)
    low = (x - high.astype(F32)).astype(BF16)
    return high, low


def dot(a, b):
    return jnp.dot(a, b, preferred_element_type=F32)


def dot3(x, w_high, w_low):
    high, low = split(x)
    return dot(high, w_high) + (dot(high, w_low) + dot(low, w_high))


def tensor_kernel(rows, total_rows, tiles, width, halos, *refs):
    where_ref = refs[0]
    blocks, refs = refs[1:10], refs[10:]
    if halos:
        up, down = refs[:2]
        refs = refs[2:]
    taps, wd_high, wd_low, wg_high, wg_low, ws_high, ws_low = refs[:7]
    outs = refs[7 : 7 + (2 if halos else 1)]
    raw_high, raw_low, pre_high, pre_low, grads, part, ty = refs[-7:]
    count = len(tiles)
    planes = 8 * count
    device = where_ref[0]
    side = 1 - 2 * lax.rem(device, 2)
    outer = rows + 2 * HALF
    trim = 4 * rows - REACH
    places = [0, side, -2, 2, side - 2, side + 2, -4, 4, -3 * side]
    starts = [n * rows for n in range(6)]
    starts += [6 * rows - trim, 7 * rows - trim, 8 * rows - 2 * trim]
    span = 3 * 8
    for n, plane in enumerate(tiles):
        for block, place, start in zip(blocks, places, starts):
            low_plane, high_plane = plane - 8, plane + 16
            if low_plane < 0:
                x = jnp.concatenate([up[start : start + rows], block[:, :high_plane]], axis=1)
            elif high_plane > block.shape[1]:
                x = jnp.concatenate([block[:, low_plane:], down[start : start + rows]], axis=1)
            else:
                x = block[:, low_plane:high_plane]
            high, low = split(x.reshape(rows * span, width))
            at = pl.ds(pl.multiple_of((place + 4) * (rows * span), 16), rows * span)
            raw_high[n, at, :] = high
            raw_low[n, at, :] = low

    group = 8
    size = group * 8
    reach = (group + 2 * GHALF) * span
    for n in range(count):
        for start in range(0, outer, group):
            at = (start + trim) * span
            high, low = raw_high[n, at : at + reach, :], raw_low[n, at : at + reach, :]
            both = dot(taps[...], high)
            result = both[: 3 * size] + (both[3 * size :] + dot(taps[: 3 * size, :], low))
            first = device * rows + (start - HALF)
            row = first + lax.broadcasted_iota(jnp.int32, (size, width), 0) // 8
            inside = jnp.logical_and(row >= 0, row < total_rows).astype(F32)
            to = n * outer * 8 + start * 8
            for f in range(3):
                high, low = split(result[f * size : (f + 1) * size] * inside)
                pre_high[f, to : to + size, :] = high
                pre_low[f, to : to + size, :] = low
    for f, (w_high, w_low) in enumerate(
        ((wd_high, wd_low), (wg_high, wg_low), (wg_high, wg_low))
    ):
        for n in range(count):
            at = slice(n * outer * 8, (n + 1) * outer * 8)
            high, low = pre_high[f, at, :], pre_low[f, at, :]
            result = dot(high, w_high[...]) + (dot(high, w_low[...]) + dot(low, w_high[...]))
            grads[f, at, :] = result

    def products(j, at, lanes):
        x, y, z = (grads[f, pl.ds(at + 8 * j, 8), lanes] for f in range(3))
        return [x * x, y * y, z * z, x * y, x * z, y * z]

    for lane in range(0, width, 128):
        lanes = slice(lane, lane + 128)

        def average_rows(t, carry, lane=lane, lanes=lanes):
            at = pl.multiple_of(t * (outer * 8), 8)
            state = products(0, at, lanes)
            for j in range(1, HALF + 1):
                state = [DECAY * s + v for s, v in zip(state, products(j, at, lanes))]
            for f in range(6):
                part[f, 0] = state[f]
            for i in range(1, rows):
                new, old = products(HALF + i, at, lanes), products(i - 1, at, lanes)
                state = [DECAY * s + (v - CUT * w) for s, v, w in zip(state, new, old)]
                for f in range(6):
                    part[f, i] = state[f]
            state = [DECAY * v for v in products(outer - 1, at, lanes)]
            for j in range(outer - 2, HALF + rows - 1, -1):
                state = [DECAY * (s + v) for s, v in zip(state, products(j, at, lanes))]
            for i in range(rows - 1, -1, -1):
                for f in range(6):
                    ty[lane // 128, f, pl.ds(t * 8 * rows + i, 8, stride=rows), :] = part[f, i] + state[f]
                if i:
                    near, far_row = products(HALF + i, at, lanes), products(2 * HALF + i, at, lanes)
                    state = [
                        DECAY * (s + v) - CUT * w for s, v, w in zip(state, near, far_row)
                    ]
            return carry

        lax.fori_loop(0, count, average_rows, 0)

    for f in range(6):
        held = jnp.concatenate([ty[h, f] for h in range(width // 128)], axis=1)
        field = dot3(held, ws_high[...], ws_low[...]).reshape(planes, rows, width)
        step = planes // len(outs)
        for n, out in enumerate(outs):
            out[:, f] = field[n * step : (n + 1) * step]


def attribute_kernel(planes, width, pieces, *refs):
    inline, cross, coherent, part = refs[-4:]
    for lane in range(0, width, 128):
        lanes = slice(lane, lane + 128)

        def plane(z):
            for ref, start in zip(refs, pieces):
                if start <= z < start + ref.shape[0]:
                    return [ref[z - start, f, :, lanes] for f in range(6)]

        state = plane(-HALF)
        for z in range(-HALF + 1, 1):
            state = [DECAY * s + v for s, v in zip(state, plane(z))]
        for f in range(6):
            part[0, f] = state[f]
        for z in range(1, planes):
            new, old = plane(z), plane(z - HALF - 1)
            state = [DECAY * s + (v - CUT * w) for s, v, w in zip(state, new, old)]
            for f in range(6):
                part[z, f] = state[f]
        state = [DECAY * v for v in plane(planes + HALF - 1)]
        for z in range(planes + HALF - 2, planes - 1, -1):
            state = [DECAY * (s + v) for s, v in zip(state, plane(z))]
        for z in range(planes - 1, -1, -1):
            xx, yy, zz, xy, xz, yz = [part[z, f] + state[f] for f in range(6)]
            scale = -1.0 / (zz + EPSILON)
            inline[z, :, lanes] = xz * scale
            cross[z, :, lanes] = yz * scale
            trace = xx + yy + zz
            minors = xx * yy + xx * zz + yy * zz - xy * xy - xz * xz - yz * yz
            coherent[z, :, lanes] = 1.0 - 3.0 * minors / (trace * trace + EPSILON)
            if z:
                near, far_plane = plane(z), plane(z + HALF)
                state = [DECAY * (s + v) - CUT * w for s, v, w in zip(state, near, far_plane)]


def send(x, axis, target):
    devices = lax.axis_size(axis)
    pairs = [(i, target(i)) for i in range(devices) if 0 <= target(i) < devices]
    return lax.ppermute(x, axis, pairs)


def local(volume):
    planes, rows, width = volume.shape
    groups = lax.axis_size("pa")
    device = lax.axis_index("pa")
    even = lax.rem(device, 2) == 0
    trim = 4 * rows - REACH
    halo = 8
    own = volume.transpose(1, 0, 2)
    above = send(own, "pa", lambda i: i + 2)
    below = send(own, "pa", lambda i: i - 2)
    other = send(own, "pa", lambda i: i ^ 1)
    above_far = send(above, "pa", lambda i: i + 2)
    below_far = send(below, "pa", lambda i: i - 2)
    above_other = send(other, "pa", lambda i: i + 2)
    below_other = send(other, "pa", lambda i: i - 2)
    last_far = send(jnp.where(even, below_far, above_far), "pa", lambda i: i ^ 1)
    pieces = [own, other, above, below, above_other, below_other, above_far, below_far, last_far]
    held = pieces[:6] + [above_far[trim:], below_far[: rows - trim], last_far]
    up = send(jnp.concatenate([x[:, planes - halo :] for x in held], axis=0), "gz", lambda i: i + 1)
    down = send(jnp.concatenate([x[:, :halo] for x in held], axis=0), "gz", lambda i: i - 1)

    weights = []
    for matrix in (
        inline_matrix(SLOPE, width), inline_matrix(SMOOTH, width), average_matrix(width)
    ):
        weights += [jnp.asarray(w) for w in split_constant(matrix)]
    matrix = np.concatenate(split_constant(tile_matrix(8, 8)), axis=0)
    weights = [jnp.asarray(matrix)] + weights
    outer = rows + 2 * HALF

    def tensors(tiles, halos, name):
        used = 8 * len(tiles)
        outs = 2 if halos else 1
        operands = pieces + (list(halos) if halos else []) + weights
        return pl.pallas_call(
            functools.partial(
                tensor_kernel, rows, rows * groups, tiles, width, bool(halos)
            ),
            out_shape=[jax.ShapeDtypeStruct((used // outs, 6, rows, width), F32)] * outs,
            in_specs=[pl.BlockSpec(memory_space=pltpu.SMEM)] + [whole] * len(operands),
            out_specs=[whole] * outs,
            scratch_shapes=[
                pltpu.VMEM((len(tiles), 9 * rows * 24, width), BF16),
                pltpu.VMEM((len(tiles), 9 * rows * 24, width), BF16),
                pltpu.VMEM((3, outer * used, width), BF16),
                pltpu.VMEM((3, outer * used, width), BF16),
                pltpu.VMEM((3, outer * used, width), F32),
                pltpu.VMEM((6, rows, 8, 128), F32),
                pltpu.VMEM((width // 128, 6, used * rows, 128), F32),
            ],
            compiler_params=pltpu.CompilerParams(vmem_limit_bytes=28 * 2**20),
            cost_estimate=pl.CostEstimate(
                flops=8 * 10**9, bytes_accessed=4 * 2**20, transcendentals=0
            ),
            name=name,
        )(device.reshape(1), *operands)

    whole = pl.BlockSpec(memory_space=pltpu.VMEM)
    (middle,) = tensors([8, 16], None, "tensor_middle")
    middle_above = send(middle, "gz", lambda i: i + 1)
    middle_below = send(middle, "gz", lambda i: i - 1)
    first, last = tensors([0, 24], (up, down), "tensor_ends")
    last_above = send(last, "gz", lambda i: i + 1)
    first_below = send(first, "gz", lambda i: i - 1)
    arrays = [middle_above, last_above, first, middle, last, first_below, middle_below]
    starts = [-HALF, -halo, 0, halo, planes - halo, planes, planes + halo]
    shape = jax.ShapeDtypeStruct((planes, rows, width), F32)
    return tuple(
        pl.pallas_call(
            functools.partial(attribute_kernel, planes, width, starts),
            out_shape=[shape] * 3,
            in_specs=[whole] * len(arrays),
            out_specs=[whole] * 3,
            scratch_shapes=[pltpu.VMEM((planes, 6, 8, 128), F32)],
            compiler_params=pltpu.CompilerParams(vmem_limit_bytes=28 * 2**20),
            name="attributes",
        )(*arrays)
    )


def solution(mesh):
    placed = P("gz", "pa", None)
    return jax.shard_map(
        local,
        mesh=mesh,
        in_specs=(placed,),
        out_specs=(placed, placed, placed),
        check_vma=False,
    )
```

```python
import functools
import math

import jax
import jax.numpy as jnp
import numpy as np
from jax import lax
from jax.experimental import pallas as pl
from jax.experimental.pallas import tpu as pltpu
from jax.sharding import PartitionSpec as P

HALF = 24
GHALF = 6
SIGMA_GRADIENT = 1.5
DECAY_LENGTH = 4.0
EPSILON = 1e-06

REACH = HALF + GHALF
DECAY = math.exp(-1.0 / DECAY_LENGTH)
CUT = math.exp(-(HALF + 1) / DECAY_LENGTH)
BF16 = jnp.bfloat16
F32 = jnp.float32


def gradient_taps():
    k = np.arange(-GHALF, GHALF + 1).astype(np.float64)
    bell = np.exp(-k * k / (2.0 * SIGMA_GRADIENT**2))
    smooth = bell / np.sqrt(np.sum(bell * bell))
    slope = k * bell / np.sqrt(np.sum((k * bell) ** 2))
    return smooth, slope


def average_scale():
    k = np.arange(-HALF, HALF + 1).astype(np.float64)
    return 1.0 / np.sum(np.exp(-np.abs(k) / DECAY_LENGTH))


SMOOTH, SLOPE = gradient_taps()


def split_constant(matrix):
    matrix = matrix.astype(np.float32)
    high = matrix.astype(BF16)
    low = (matrix - high.astype(np.float32)).astype(BF16)
    return high, low


def inline_matrix(taps, length):
    reach = (len(taps) - 1) // 2
    offset = np.arange(length)[:, None] - np.arange(length)[None, :]
    inside = np.abs(offset) <= reach
    return np.where(inside, taps[np.clip(offset + reach, 0, 2 * reach)], 0.0)


def average_matrix(length):
    offset = np.abs(np.arange(length)[:, None] - np.arange(length)[None, :])
    values = np.exp(-offset / DECAY_LENGTH) * average_scale() ** 3
    return np.where(offset <= HALF, values, 0.0)


def tile_matrix(rows, planes):
    def band(taps, outputs, inputs, lead):
        offset = np.arange(inputs)[None, :] - np.arange(outputs)[:, None] - lead
        inside = np.abs(offset) <= GHALF
        return np.where(inside, taps[np.clip(offset + GHALF, 0, 2 * GHALF)], 0.0)

    def pair(cross, depth):
        cross = band(cross, rows, rows + 2 * GHALF, GHALF)
        depth = band(depth, planes, 3 * planes, planes)
        return np.kron(cross, depth)

    return np.concatenate(
        [pair(SMOOTH, SMOOTH), pair(SLOPE, SMOOTH), pair(SMOOTH, SLOPE)], axis=0
    )


def split(x):
    high = x.astype(BF16)
    low = (x - high.astype(F32)).astype(BF16)
    return high, low


def dot(a, b):
    return jnp.dot(a, b, preferred_element_type=F32)


def dot3(x, w_high, w_low):
    high, low = split(x)
    return dot(high, w_high) + (dot(high, w_low) + dot(low, w_high))


def tensor_kernel(rows, total_rows, tiles, width, halos, *refs):
    blocks, refs = refs[:9], refs[9:]
    if halos:
        swaps, last_halo = refs[:2], refs[2]
        refs = refs[3:]
    taps, wd_high, wd_low, wg_high, wg_low, ws_high, ws_low = refs[:7]
    outs = refs[7 : 7 + (4 if halos else 1)]
    raw_high, raw_low, pre_high, pre_low, grads, part, ty = refs[-7:]
    count = len(tiles)
    planes = 8 * count
    device = lax.axis_index("pa")
    side = 1 - 2 * lax.rem(device, 2)
    even_depth = lax.rem(lax.axis_index("gz"), 2) == 0
    outer = rows + 2 * HALF
    trim = 4 * rows - REACH
    places = [0, -2, 2, side, -4, 4, side - 2, side + 2, -3 * side]
    span = 3 * 8

    def stage(n, place, x):
        high, low = split(x.reshape(rows * span, width))
        at = pl.ds(pl.multiple_of((place + 4) * (rows * span), 16), rows * span)
        raw_high[n, at, :] = high
        raw_low[n, at, :] = low

    def stage_ends(up, down):
        for i, (block, place) in enumerate(zip(blocks, places)):
            at = slice(i * rows, (i + 1) * rows)
            last = i == len(blocks) - 1
            above = last_halo[:, :8] if last else up[at]
            below = last_halo[:, 8:] if last else down[at]
            stage(0, place, jnp.concatenate([above, block[:, :16]], axis=1))
            stage(1, place, jnp.concatenate([block[:, -16:], below], axis=1))

    if halos:
        pl.when(even_depth)(lambda: stage_ends(swaps[1], swaps[0]))
        pl.when(jnp.logical_not(even_depth))(lambda: stage_ends(swaps[0], swaps[1]))
    else:
        for n, plane in enumerate(tiles):
            for block, place in zip(blocks, places):
                stage(n, place, block[:, plane - 8 : plane + 16])

    group = 8
    size = group * 8
    reach = (group + 2 * GHALF) * span
    for n in range(count):
        for start in range(0, outer, group):
            at = (start + trim) * span
            high, low = raw_high[n, at : at + reach, :], raw_low[n, at : at + reach, :]
            both = dot(taps[...], high)
            result = both[: 3 * size] + (both[3 * size :] + dot(taps[: 3 * size, :], low))
            first = device * rows + (start - HALF)
            row = first + lax.broadcasted_iota(jnp.int32, (size, width), 0) // 8
            inside = jnp.logical_and(row >= 0, row < total_rows).astype(F32)
            to = n * outer * 8 + start * 8
            for f in range(3):
                high, low = split(result[f * size : (f + 1) * size] * inside)
                pre_high[f, to : to + size, :] = high
                pre_low[f, to : to + size, :] = low
    for f, (w_high, w_low) in enumerate(
        ((wd_high, wd_low), (wg_high, wg_low), (wg_high, wg_low))
    ):
        for n in range(count):
            at = slice(n * outer * 8, (n + 1) * outer * 8)
            high, low = pre_high[f, at, :], pre_low[f, at, :]
            result = dot(high, w_high[...]) + (dot(high, w_low[...]) + dot(low, w_high[...]))
            grads[f, at, :] = result

    def products(j, at, lanes):
        x, y, z = (grads[f, pl.ds(at + 8 * j, 8), lanes] for f in range(3))
        return [x * x, y * y, z * z, x * y, x * z, y * z]

    for lane in range(0, width, 128):
        lanes = slice(lane, lane + 128)

        def average_rows(t, carry, lane=lane, lanes=lanes):
            at = pl.multiple_of(t * (outer * 8), 8)
            state = products(0, at, lanes)
            for j in range(1, HALF + 1):
                state = [DECAY * s + v for s, v in zip(state, products(j, at, lanes))]
            for f in range(6):
                part[f, 0] = state[f]
            for i in range(1, rows):
                new, old = products(HALF + i, at, lanes), products(i - 1, at, lanes)
                state = [DECAY * s + (v - CUT * w) for s, v, w in zip(state, new, old)]
                for f in range(6):
                    part[f, i] = state[f]
            state = [DECAY * v for v in products(outer - 1, at, lanes)]
            for j in range(outer - 2, HALF + rows - 1, -1):
                state = [DECAY * (s + v) for s, v in zip(state, products(j, at, lanes))]
            for i in range(rows - 1, -1, -1):
                for f in range(6):
                    ty[lane // 128, f, pl.ds(t * 8 * rows + i, 8, stride=rows), :] = part[f, i] + state[f]
                if i:
                    near, far_row = products(HALF + i, at, lanes), products(2 * HALF + i, at, lanes)
                    state = [
                        DECAY * (s + v) - CUT * w for s, v, w in zip(state, near, far_row)
                    ]
            return carry

        lax.fori_loop(0, count, average_rows, 0)

    for f in range(6):
        held = jnp.concatenate([ty[h, f] for h in range(width // 128)], axis=1)
        field = dot3(held, ws_high[...], ws_low[...]).reshape(planes, rows, width)
        if not halos:
            outs[0][:, f] = field
            continue
        first, last = field[:8], field[8:]
        outs[0][:, f] = first
        outs[1][:, f] = last
        outs[2][:, f] = jnp.where(even_depth, last, first)
        outs[3][:, f] = jnp.where(even_depth, first, last)


def attribute_kernel(planes, width, pieces, *refs):
    inline, cross, coherent, part = refs[-4:]
    first, middle, last, ends_a, middle_a, ends_b, middle_b = refs[:7]
    even_depth = lax.rem(lax.axis_index("gz"), 2) == 0
    results = (inline, cross, coherent, part)
    own = (first, middle, last)
    pl.when(even_depth)(
        lambda: attributes(
            planes, width, pieces, (middle_b, ends_b, *own, ends_a, middle_a), *results
        )
    )
    pl.when(jnp.logical_not(even_depth))(
        lambda: attributes(
            planes, width, pieces, (middle_a, ends_a, *own, ends_b, middle_b), *results
        )
    )


def attributes(planes, width, pieces, refs, inline, cross, coherent, part):
    for lane in range(0, width, 128):
        lanes = slice(lane, lane + 128)

        def plane(z):
            for ref, start in zip(refs, pieces):
                if start <= z < start + ref.shape[0]:
                    return [ref[z - start, f, :, lanes] for f in range(6)]

        state = plane(-HALF)
        for z in range(-HALF + 1, 1):
            state = [DECAY * s + v for s, v in zip(state, plane(z))]
        for f in range(6):
            part[0, f] = state[f]
        for z in range(1, planes):
            new, old = plane(z), plane(z - HALF - 1)
            state = [DECAY * s + (v - CUT * w) for s, v, w in zip(state, new, old)]
            for f in range(6):
                part[z, f] = state[f]
        state = [DECAY * v for v in plane(planes + HALF - 1)]
        for z in range(planes + HALF - 2, planes - 1, -1):
            state = [DECAY * (s + v) for s, v in zip(state, plane(z))]
        for z in range(planes - 1, -1, -1):
            xx, yy, zz, xy, xz, yz = [part[z, f] + state[f] for f in range(6)]
            scale = -1.0 / (zz + EPSILON)
            inline[z, :, lanes] = xz * scale
            cross[z, :, lanes] = yz * scale
            trace = xx + yy + zz
            minors = xx * yy + xx * zz + yy * zz - xy * xy - xz * xz - yz * yz
            coherent[z, :, lanes] = 1.0 - 3.0 * minors / (trace * trace + EPSILON)
            if z:
                near, far_plane = plane(z), plane(z + HALF)
                state = [DECAY * (s + v) - CUT * w for s, v, w in zip(state, near, far_plane)]


def send(x, axis, target):
    devices = lax.axis_size(axis)
    pairs = [(i, target(i)) for i in range(devices) if 0 <= target(i) < devices]
    return lax.ppermute(x, axis, pairs)


def local(volume):
    planes, rows, width = volume.shape
    groups = lax.axis_size("pa")
    device = lax.axis_index("pa")
    depth = lax.rem(lax.axis_index("gz"), 2)
    turn = lax.rem(device, 2) == lax.rem(device // 2, 2)
    halo = 8

    def cross(x):
        return send(x, "pa", lambda i: i ^ 1)

    def near(x):
        return send(x, "pa", lambda i: i ^ 2)

    def away(x):
        return send(x, "pa", lambda i: i - 2 if i % 4 < 2 else i + 2)

    def depth_swaps(even_near, even_away):
        one = send(even_near, "gz", lambda i: i ^ 1)
        two = send(even_away, "gz", lambda i: i - 1 if i % 2 == 0 else i + 1)
        return one, two

    def ordered(one, two):
        return jnp.where(low, two, one), jnp.where(low, one, two)

    low = lax.rem(device // 2, 2) == 0
    own = volume.transpose(1, 0, 2)
    near_own, away_own, other = near(own), away(own), cross(own)
    near_far, away_far = near(away_own), away(near_own)
    near_other, away_other = near(other), away(other)
    last_far = cross(jnp.where(turn, near_far, away_far))
    pieces = [own, *ordered(near_own, away_own), other, *ordered(near_far, away_far)]
    pieces += ordered(near_other, away_other)
    last_planes = jnp.concatenate([x[:, planes - halo :] for x in pieces], axis=0)
    first_planes = jnp.concatenate([x[:, :halo] for x in pieces], axis=0)
    even = depth == 0
    swaps = depth_swaps(
        jnp.where(even, last_planes, first_planes), jnp.where(even, first_planes, last_planes)
    )
    pieces.append(last_far)

    weights = []
    for matrix in (
        inline_matrix(SLOPE, width), inline_matrix(SMOOTH, width), average_matrix(width)
    ):
        weights += [jnp.asarray(w) for w in split_constant(matrix)]
    matrix = np.concatenate(split_constant(tile_matrix(8, 8)), axis=0)
    weights = [jnp.asarray(matrix)] + weights
    outer = rows + 2 * HALF

    def tensors(tiles, halos, name):
        used = 8 * len(tiles)
        outs = 4 if halos else 1
        count = 8 if halos else used
        operands = pieces + (list(halos) if halos else []) + weights
        return pl.pallas_call(
            functools.partial(
                tensor_kernel, rows, rows * groups, tiles, width, bool(halos)
            ),
            out_shape=[jax.ShapeDtypeStruct((count, 6, rows, width), F32)] * outs,
            in_specs=[whole] * len(operands),
            out_specs=[whole] * outs,
            scratch_shapes=[
                pltpu.VMEM((len(tiles), 9 * rows * 24, width), BF16),
                pltpu.VMEM((len(tiles), 9 * rows * 24, width), BF16),
                pltpu.VMEM((3, outer * used, width), BF16),
                pltpu.VMEM((3, outer * used, width), BF16),
                pltpu.VMEM((3, outer * used, width), F32),
                pltpu.VMEM((6, rows, 8, 128), F32),
                pltpu.VMEM((width // 128, 6, used * rows, 128), F32),
            ],
            compiler_params=pltpu.CompilerParams(vmem_limit_bytes=28 * 2**20),
            cost_estimate=pl.CostEstimate(
                flops=8 * 10**9, bytes_accessed=4 * 2**20, transcendentals=0
            ),
            name=name,
        )(*operands)

    whole = pl.BlockSpec(memory_space=pltpu.VMEM)
    (middle,) = tensors([8, 16], None, "tensor_middle")
    middle, *swaps = lax.optimization_barrier((middle, *swaps))
    at, beyond = 4 * rows, 5 * rows
    kept = lax.rem(device, 2) == 0
    chosen = [jnp.where(kept, x[beyond : beyond + rows], x[at:beyond]) for x in swaps]
    last_halo = cross(
        jnp.concatenate(
            [
                jnp.where(even, chosen[1], chosen[0]),
                jnp.where(even, chosen[0], chosen[1]),
            ],
            axis=1,
        )
    )
    middle_swaps = depth_swaps(middle, middle)
    first, last, even_near, even_away = tensors([0, 24], (*swaps, last_halo), "tensor_ends")
    end_swaps = depth_swaps(even_near, even_away)
    arrays = [first, middle, last, end_swaps[0], middle_swaps[0], end_swaps[1], middle_swaps[1]]
    starts = [-HALF, -halo, 0, halo, planes - halo, planes, planes + halo]
    shape = jax.ShapeDtypeStruct((planes, rows, width), F32)
    return tuple(
        pl.pallas_call(
            functools.partial(attribute_kernel, planes, width, starts),
            out_shape=[shape] * 3,
            in_specs=[whole] * len(arrays),
            out_specs=[whole] * 3,
            scratch_shapes=[pltpu.VMEM((planes, 6, 8, 128), F32)],
            compiler_params=pltpu.CompilerParams(vmem_limit_bytes=28 * 2**20),
            name="attributes",
        )(*arrays)
    )


def solution(mesh):
    placed = P("gz", "pa", None)
    return jax.shard_map(
        local,
        mesh=mesh,
        in_specs=(placed,),
        out_specs=(placed, placed, placed),
        check_vma=False,
    )
```

```python
import functools
import math

import jax
import jax.numpy as jnp
import numpy as np
from jax import lax
from jax.experimental import pallas as pl
from jax.experimental.pallas import tpu as pltpu
from jax.sharding import PartitionSpec as P

HALF = 24
GHALF = 6
SIGMA_GRADIENT = 1.5
DECAY_LENGTH = 4.0
EPSILON = 1e-06

REACH = HALF + GHALF
DECAY = math.exp(-1.0 / DECAY_LENGTH)
CUT = math.exp(-(HALF + 1) / DECAY_LENGTH)
BF16 = jnp.bfloat16
F32 = jnp.float32


def gradient_taps():
    k = np.arange(-GHALF, GHALF + 1).astype(np.float64)
    bell = np.exp(-k * k / (2.0 * SIGMA_GRADIENT**2))
    smooth = bell / np.sqrt(np.sum(bell * bell))
    slope = k * bell / np.sqrt(np.sum((k * bell) ** 2))
    return smooth, slope


def average_scale():
    k = np.arange(-HALF, HALF + 1).astype(np.float64)
    return 1.0 / np.sum(np.exp(-np.abs(k) / DECAY_LENGTH))


SMOOTH, SLOPE = gradient_taps()


def split_constant(matrix):
    matrix = matrix.astype(np.float32)
    high = matrix.astype(BF16)
    low = (matrix - high.astype(np.float32)).astype(BF16)
    return high, low


def inline_matrix(taps, length):
    reach = (len(taps) - 1) // 2
    offset = np.arange(length)[:, None] - np.arange(length)[None, :]
    inside = np.abs(offset) <= reach
    return np.where(inside, taps[np.clip(offset + reach, 0, 2 * reach)], 0.0)


def average_matrix(length):
    offset = np.abs(np.arange(length)[:, None] - np.arange(length)[None, :])
    values = np.exp(-offset / DECAY_LENGTH) * average_scale() ** 3
    return np.where(offset <= HALF, values, 0.0)


def tile_matrix(rows, planes):
    def band(taps, outputs, inputs, lead):
        offset = np.arange(inputs)[None, :] - np.arange(outputs)[:, None] - lead
        inside = np.abs(offset) <= GHALF
        return np.where(inside, taps[np.clip(offset + GHALF, 0, 2 * GHALF)], 0.0)

    def pair(cross, depth):
        cross = band(cross, rows, rows + 2 * GHALF, GHALF)
        depth = band(depth, planes, 3 * planes, planes)
        return np.kron(cross, depth)

    return np.concatenate(
        [pair(SMOOTH, SMOOTH), pair(SLOPE, SMOOTH), pair(SMOOTH, SLOPE)], axis=0
    )


def split(x):
    high = x.astype(BF16)
    low = (x - high.astype(F32)).astype(BF16)
    return high, low


def dot(a, b):
    return jnp.dot(a, b, preferred_element_type=F32)


def dot3(x, w_high, w_low):
    high, low = split(x)
    return dot(high, w_high) + (dot(high, w_low) + dot(low, w_high))


def tensor_kernel(rows, total_rows, tiles, width, halos, *refs):
    blocks, refs = refs[:9], refs[9:]
    if halos:
        halo, refs = refs[0], refs[1:]
    taps, wd_high, wd_low, wg_high, wg_low, ws_high, ws_low = refs[:7]
    out = refs[7]
    raw_high, raw_low, pre_high, pre_low, grads, part, ty = refs[-7:]
    count = len(tiles)
    planes = 8 * count
    device = lax.axis_index("pa")
    side = 1 - 2 * lax.rem(device, 2)
    even_depth = lax.rem(lax.axis_index("gz"), 2) == 0
    outer = rows + 2 * HALF
    trim = 4 * rows - REACH
    places = [0, -2, 2, side, -4, 4, side - 2, side + 2, -3 * side]
    span = 3 * 8

    def stage(n, place, x):
        high, low = split(x.reshape(rows * span, width))
        at = pl.ds(pl.multiple_of((place + 4) * (rows * span), 16), rows * span)
        raw_high[n, at, :] = high
        raw_low[n, at, :] = low

    def stage_end(first):
        for i, (block, place) in enumerate(zip(blocks, places)):
            beyond = halo[i * rows : (i + 1) * rows]
            parts = [beyond, block[:, :16]] if first else [block[:, -16:], beyond]
            stage(0, place, jnp.concatenate(parts, axis=1))

    if halos:
        upper = even_depth if halos == "away" else jnp.logical_not(even_depth)
        pl.when(upper)(lambda: stage_end(True))
        pl.when(jnp.logical_not(upper))(lambda: stage_end(False))
    else:
        for n, plane in enumerate(tiles):
            for block, place in zip(blocks, places):
                stage(n, place, block[:, plane - 8 : plane + 16])

    group = 8
    size = group * 8
    reach = (group + 2 * GHALF) * span
    for n in range(count):
        for start in range(0, outer, group):
            at = (start + trim) * span
            high, low = raw_high[n, at : at + reach, :], raw_low[n, at : at + reach, :]
            both = dot(taps[...], high)
            result = both[: 3 * size] + (both[3 * size :] + dot(taps[: 3 * size, :], low))
            first = device * rows + (start - HALF)
            row = first + lax.broadcasted_iota(jnp.int32, (size, width), 0) // 8
            inside = jnp.logical_and(row >= 0, row < total_rows).astype(F32)
            to = n * outer * 8 + start * 8
            for f in range(3):
                high, low = split(result[f * size : (f + 1) * size] * inside)
                pre_high[f, to : to + size, :] = high
                pre_low[f, to : to + size, :] = low
    for f, (w_high, w_low) in enumerate(
        ((wd_high, wd_low), (wg_high, wg_low), (wg_high, wg_low))
    ):
        for n in range(count):
            at = slice(n * outer * 8, (n + 1) * outer * 8)
            high, low = pre_high[f, at, :], pre_low[f, at, :]
            result = dot(high, w_high[...]) + (dot(high, w_low[...]) + dot(low, w_high[...]))
            grads[f, at, :] = result

    def products(j, at, lanes):
        x, y, z = (grads[f, pl.ds(at + 8 * j, 8), lanes] for f in range(3))
        return [x * x, y * y, z * z, x * y, x * z, y * z]

    for lane in range(0, width, 128):
        lanes = slice(lane, lane + 128)

        def average_rows(t, carry, lane=lane, lanes=lanes):
            at = pl.multiple_of(t * (outer * 8), 8)
            state = products(0, at, lanes)
            for j in range(1, HALF + 1):
                state = [DECAY * s + v for s, v in zip(state, products(j, at, lanes))]
            for f in range(6):
                part[f, 0] = state[f]
            for i in range(1, rows):
                new, old = products(HALF + i, at, lanes), products(i - 1, at, lanes)
                state = [DECAY * s + (v - CUT * w) for s, v, w in zip(state, new, old)]
                for f in range(6):
                    part[f, i] = state[f]
            state = [DECAY * v for v in products(outer - 1, at, lanes)]
            for j in range(outer - 2, HALF + rows - 1, -1):
                state = [DECAY * (s + v) for s, v in zip(state, products(j, at, lanes))]
            for i in range(rows - 1, -1, -1):
                for f in range(6):
                    ty[lane // 128, f, pl.ds(t * 8 * rows + i, 8, stride=rows), :] = part[f, i] + state[f]
                if i:
                    near, far_row = products(HALF + i, at, lanes), products(2 * HALF + i, at, lanes)
                    state = [
                        DECAY * (s + v) - CUT * w for s, v, w in zip(state, near, far_row)
                    ]
            return carry

        lax.fori_loop(0, count, average_rows, 0)

    for f in range(6):
        held = jnp.concatenate([ty[h, f] for h in range(width // 128)], axis=1)
        field = dot3(held, ws_high[...], ws_low[...]).reshape(planes, rows, width)
        out[:, f] = field


def attribute_kernel(planes, width, pieces, *refs):
    inline, cross, coherent, part = refs[-4:]
    middle, end_near, end_away, ends_a, middle_a, ends_b, middle_b = refs[:7]
    even_depth = lax.rem(lax.axis_index("gz"), 2) == 0
    results = (inline, cross, coherent, part)
    pl.when(even_depth)(
        lambda: attributes(
            planes, width, pieces,
            (middle_b, ends_b, end_away, middle, end_near, ends_a, middle_a), *results
        )
    )
    pl.when(jnp.logical_not(even_depth))(
        lambda: attributes(
            planes, width, pieces,
            (middle_a, ends_a, end_near, middle, end_away, ends_b, middle_b), *results
        )
    )


def attributes(planes, width, pieces, refs, inline, cross, coherent, part):
    for lane in range(0, width, 128):
        lanes = slice(lane, lane + 128)

        def plane(z):
            for ref, start in zip(refs, pieces):
                if start <= z < start + ref.shape[0]:
                    return [ref[z - start, f, :, lanes] for f in range(6)]

        state = plane(-HALF)
        for z in range(-HALF + 1, 1):
            state = [DECAY * s + v for s, v in zip(state, plane(z))]
        for f in range(6):
            part[0, f] = state[f]
        for z in range(1, planes):
            new, old = plane(z), plane(z - HALF - 1)
            state = [DECAY * s + (v - CUT * w) for s, v, w in zip(state, new, old)]
            for f in range(6):
                part[z, f] = state[f]
        state = [DECAY * v for v in plane(planes + HALF - 1)]
        for z in range(planes + HALF - 2, planes - 1, -1):
            state = [DECAY * (s + v) for s, v in zip(state, plane(z))]
        for z in range(planes - 1, -1, -1):
            xx, yy, zz, xy, xz, yz = [part[z, f] + state[f] for f in range(6)]
            scale = -1.0 / (zz + EPSILON)
            inline[z, :, lanes] = xz * scale
            cross[z, :, lanes] = yz * scale
            trace = xx + yy + zz
            minors = xx * yy + xx * zz + yy * zz - xy * xy - xz * xz - yz * yz
            coherent[z, :, lanes] = 1.0 - 3.0 * minors / (trace * trace + EPSILON)
            if z:
                near, far_plane = plane(z), plane(z + HALF)
                state = [DECAY * (s + v) - CUT * w for s, v, w in zip(state, near, far_plane)]


def send(x, axis, target):
    devices = lax.axis_size(axis)
    pairs = [(i, target(i)) for i in range(devices) if 0 <= target(i) < devices]
    return lax.ppermute(x, axis, pairs)


def local(volume):
    planes, rows, width = volume.shape
    groups = lax.axis_size("pa")
    device = lax.axis_index("pa")
    depth = lax.rem(lax.axis_index("gz"), 2)
    turn = lax.rem(device, 2) == lax.rem(device // 2, 2)
    halo = 8

    def cross(x):
        return send(x, "pa", lambda i: i ^ 1)

    def near(x):
        return send(x, "pa", lambda i: i ^ 2)

    def away(x):
        return send(x, "pa", lambda i: i - 2 if i % 4 < 2 else i + 2)

    def depth_near(x):
        return send(x, "gz", lambda i: i ^ 1)

    def depth_away(x):
        return send(x, "gz", lambda i: i - 1 if i % 2 == 0 else i + 1)

    def ordered(one, two):
        return jnp.where(low, two, one), jnp.where(low, one, two)

    low = lax.rem(device // 2, 2) == 0
    own = volume.transpose(1, 0, 2)
    near_own, away_own, other = near(own), away(own), cross(own)
    near_far, away_far = near(away_own), away(near_own)
    near_other, away_other = near(other), away(other)
    last_far = cross(jnp.where(turn, near_far, away_far))
    pieces = [own, *ordered(near_own, away_own), other, *ordered(near_far, away_far)]
    pieces += [*ordered(near_other, away_other), last_far]
    last_planes = jnp.concatenate([x[:, planes - halo :] for x in pieces], axis=0)
    first_planes = jnp.concatenate([x[:, :halo] for x in pieces], axis=0)
    even = depth == 0
    swap_away = depth_away(jnp.where(even, first_planes, last_planes))
    swap_near = depth_near(jnp.where(even, last_planes, first_planes))

    weights = []
    for matrix in (
        inline_matrix(SLOPE, width), inline_matrix(SMOOTH, width), average_matrix(width)
    ):
        weights += [jnp.asarray(w) for w in split_constant(matrix)]
    matrix = np.concatenate(split_constant(tile_matrix(8, 8)), axis=0)
    weights = [jnp.asarray(matrix)] + weights
    outer = rows + 2 * HALF

    def tensors(tiles, halos, kind, name):
        used = 8 * len(tiles)
        operands = pieces + halos + weights
        return pl.pallas_call(
            functools.partial(
                tensor_kernel, rows, rows * groups, tiles, width, kind
            ),
            out_shape=jax.ShapeDtypeStruct((used, 6, rows, width), F32),
            in_specs=[whole] * len(operands),
            out_specs=whole,
            scratch_shapes=[
                pltpu.VMEM((len(tiles), 9 * rows * 24, width), BF16),
                pltpu.VMEM((len(tiles), 9 * rows * 24, width), BF16),
                pltpu.VMEM((3, outer * used, width), BF16),
                pltpu.VMEM((3, outer * used, width), BF16),
                pltpu.VMEM((3, outer * used, width), F32),
                pltpu.VMEM((6, rows, 8, 128), F32),
                pltpu.VMEM((width // 128, 6, used * rows, 128), F32),
            ],
            compiler_params=pltpu.CompilerParams(vmem_limit_bytes=28 * 2**20),
            cost_estimate=pl.CostEstimate(
                flops=8 * 10**9, bytes_accessed=4 * 2**20, transcendentals=0
            ),
            name=name,
        )(*operands)

    whole = pl.BlockSpec(memory_space=pltpu.VMEM)
    middle = tensors([8, 16], [], None, "tensor_middle")
    middle_away = depth_away(middle)
    middle_near = depth_near(middle)
    end_away = tensors([0], [swap_away], "away", "tensor_away")
    from_away = depth_away(end_away)
    end_near = tensors([0], [swap_near], "near", "tensor_near")
    from_near = depth_near(end_near)
    arrays = [middle, end_near, end_away, from_near, middle_near, from_away, middle_away]
    starts = [-HALF, -halo, 0, halo, planes - halo, planes, planes + halo]
    shape = jax.ShapeDtypeStruct((planes, rows, width), F32)
    return tuple(
        pl.pallas_call(
            functools.partial(attribute_kernel, planes, width, starts),
            out_shape=[shape] * 3,
            in_specs=[whole] * len(arrays),
            out_specs=[whole] * 3,
            scratch_shapes=[pltpu.VMEM((planes, 6, 8, 128), F32)],
            compiler_params=pltpu.CompilerParams(vmem_limit_bytes=28 * 2**20),
            name="attributes",
        )(*arrays)
    )


def solution(mesh):
    placed = P("gz", "pa", None)
    return jax.shard_map(
        local,
        mesh=mesh,
        in_specs=(placed,),
        out_specs=(placed, placed, placed),
        check_vma=False,
    )
```

```python
import functools
import math

import jax
import jax.numpy as jnp
import numpy as np
from jax import lax
from jax.experimental import pallas as pl
from jax.experimental.pallas import tpu as pltpu
from jax.sharding import PartitionSpec as P

HALF = 24
GHALF = 6
SIGMA_GRADIENT = 1.5
DECAY_LENGTH = 4.0
EPSILON = 1e-06

REACH = HALF + GHALF
DECAY = math.exp(-1.0 / DECAY_LENGTH)
CUT = math.exp(-(HALF + 1) / DECAY_LENGTH)
BF16 = jnp.bfloat16
F32 = jnp.float32


def gradient_taps():
    k = np.arange(-GHALF, GHALF + 1).astype(np.float64)
    bell = np.exp(-k * k / (2.0 * SIGMA_GRADIENT**2))
    smooth = bell / np.sqrt(np.sum(bell * bell))
    slope = k * bell / np.sqrt(np.sum((k * bell) ** 2))
    return smooth, slope


def average_scale():
    k = np.arange(-HALF, HALF + 1).astype(np.float64)
    return 1.0 / np.sum(np.exp(-np.abs(k) / DECAY_LENGTH))


SMOOTH, SLOPE = gradient_taps()


def split_constant(matrix):
    matrix = matrix.astype(np.float32)
    high = matrix.astype(BF16)
    low = (matrix - high.astype(np.float32)).astype(BF16)
    return high, low


def inline_matrix(taps, length):
    reach = (len(taps) - 1) // 2
    offset = np.arange(length)[:, None] - np.arange(length)[None, :]
    inside = np.abs(offset) <= reach
    return np.where(inside, taps[np.clip(offset + reach, 0, 2 * reach)], 0.0)


def average_matrix(length):
    offset = np.abs(np.arange(length)[:, None] - np.arange(length)[None, :])
    values = np.exp(-offset / DECAY_LENGTH) * average_scale() ** 3
    return np.where(offset <= HALF, values, 0.0)


def tile_matrix(rows, planes):
    def band(taps, outputs, inputs, lead):
        offset = np.arange(inputs)[None, :] - np.arange(outputs)[:, None] - lead
        inside = np.abs(offset) <= GHALF
        return np.where(inside, taps[np.clip(offset + GHALF, 0, 2 * GHALF)], 0.0)

    def pair(cross, depth):
        cross = band(cross, rows, rows + 2 * GHALF, GHALF)
        depth = band(depth, planes, 3 * planes, planes)
        return np.kron(cross, depth)

    return np.concatenate(
        [pair(SMOOTH, SMOOTH), pair(SLOPE, SMOOTH), pair(SMOOTH, SLOPE)], axis=0
    )


def split(x):
    high = x.astype(BF16)
    low = (x - high.astype(F32)).astype(BF16)
    return high, low


def dot(a, b):
    return jnp.dot(a, b, preferred_element_type=F32)


def dot3(x, w_high, w_low):
    high, low = split(x)
    return dot(high, w_high) + (dot(high, w_low) + dot(low, w_high))


def tensor_kernel(rows, total_rows, tiles, width, halos, *refs):
    blocks, refs = refs[:9], refs[9:]
    if halos:
        count, upper_side = halos
        halo, refs = refs[:count], refs[count:]
    taps, wd_high, wd_low, wg_high, wg_low, ws_high, ws_low = refs[:7]
    out = refs[7]
    raw_high, raw_low, pre_high, pre_low, grads, part, ty = refs[-7:]
    tile_count = len(tiles)
    planes = 8 * tile_count
    device = lax.axis_index("pa")
    side = 1 - 2 * lax.rem(device, 2)
    even_depth = lax.rem(lax.axis_index("gz"), 2) == 0
    outer = rows + 2 * HALF
    trim = 4 * rows - REACH
    places = [0, -2, 2, side, -4, 4, side - 2, side + 2, -3 * side]
    span = 3 * 8

    def stage(n, place, x):
        high, low = split(x.reshape(rows * span, width))
        at = pl.ds(pl.multiple_of((place + 4) * (rows * span), 16), rows * span)
        raw_high[n, at, :] = high
        raw_low[n, at, :] = low

    def stage_end(first):
        for i, (block, place) in enumerate(zip(blocks, places)):
            part, at = (halo[0], i) if i < 4 or count == 1 else (halo[1], i - 4)
            beyond = part[at * rows : (at + 1) * rows]
            parts = [beyond, block[:, :16]] if first else [block[:, -16:], beyond]
            stage(0, place, jnp.concatenate(parts, axis=1))

    if halos:
        upper = even_depth if upper_side == "away" else jnp.logical_not(even_depth)
        pl.when(upper)(lambda: stage_end(True))
        pl.when(jnp.logical_not(upper))(lambda: stage_end(False))
    else:
        for n, plane in enumerate(tiles):
            for block, place in zip(blocks, places):
                stage(n, place, block[:, plane - 8 : plane + 16])

    group = 8
    size = group * 8
    reach = (group + 2 * GHALF) * span
    for n in range(tile_count):
        for start in range(0, outer, group):
            at = (start + trim) * span
            high, low = raw_high[n, at : at + reach, :], raw_low[n, at : at + reach, :]
            both = dot(taps[...], high)
            result = both[: 3 * size] + (both[3 * size :] + dot(taps[: 3 * size, :], low))
            first = device * rows + (start - HALF)
            row = first + lax.broadcasted_iota(jnp.int32, (size, width), 0) // 8
            inside = jnp.logical_and(row >= 0, row < total_rows).astype(F32)
            to = n * outer * 8 + start * 8
            for f in range(3):
                high, low = split(result[f * size : (f + 1) * size] * inside)
                pre_high[f, to : to + size, :] = high
                pre_low[f, to : to + size, :] = low
    for f, (w_high, w_low) in enumerate(
        ((wd_high, wd_low), (wg_high, wg_low), (wg_high, wg_low))
    ):
        for n in range(tile_count):
            at = slice(n * outer * 8, (n + 1) * outer * 8)
            high, low = pre_high[f, at, :], pre_low[f, at, :]
            result = dot(high, w_high[...]) + (dot(high, w_low[...]) + dot(low, w_high[...]))
            grads[f, at, :] = result

    def products(j, at, lanes):
        x, y, z = (grads[f, pl.ds(at + 8 * j, 8), lanes] for f in range(3))
        return [x * x, y * y, z * z, x * y, x * z, y * z]

    for lane in range(0, width, 128):
        lanes = slice(lane, lane + 128)

        def average_rows(t, carry, lane=lane, lanes=lanes):
            at = pl.multiple_of(t * (outer * 8), 8)
            state = products(0, at, lanes)
            for j in range(1, HALF + 1):
                state = [DECAY * s + v for s, v in zip(state, products(j, at, lanes))]
            for f in range(6):
                part[f, 0] = state[f]
            for i in range(1, rows):
                new, old = products(HALF + i, at, lanes), products(i - 1, at, lanes)
                state = [DECAY * s + (v - CUT * w) for s, v, w in zip(state, new, old)]
                for f in range(6):
                    part[f, i] = state[f]
            state = [DECAY * v for v in products(outer - 1, at, lanes)]
            for j in range(outer - 2, HALF + rows - 1, -1):
                state = [DECAY * (s + v) for s, v in zip(state, products(j, at, lanes))]
            for i in range(rows - 1, -1, -1):
                for f in range(6):
                    ty[lane // 128, f, pl.ds(t * 8 * rows + i, 8, stride=rows), :] = part[f, i] + state[f]
                if i:
                    near, far_row = products(HALF + i, at, lanes), products(2 * HALF + i, at, lanes)
                    state = [
                        DECAY * (s + v) - CUT * w for s, v, w in zip(state, near, far_row)
                    ]
            return carry

        lax.fori_loop(0, tile_count, average_rows, 0)

    for f in range(6):
        held = jnp.concatenate([ty[h, f] for h in range(width // 128)], axis=1)
        field = dot3(held, ws_high[...], ws_low[...]).reshape(planes, rows, width)
        out[:, f] = field


def attribute_kernel(planes, width, pieces, *refs):
    inline, cross, coherent, part = refs[-4:]
    middle, end_near, end_away, ends_a, middle_a, ends_b, middle_b = refs[:7]
    even_depth = lax.rem(lax.axis_index("gz"), 2) == 0
    results = (inline, cross, coherent, part)
    pl.when(even_depth)(
        lambda: attributes(
            planes, width, pieces,
            (middle_b, ends_b, end_away, middle, end_near, ends_a, middle_a), *results
        )
    )
    pl.when(jnp.logical_not(even_depth))(
        lambda: attributes(
            planes, width, pieces,
            (middle_a, ends_a, end_near, middle, end_away, ends_b, middle_b), *results
        )
    )


def attributes(planes, width, pieces, refs, inline, cross, coherent, part):
    for lane in range(0, width, 128):
        lanes = slice(lane, lane + 128)

        def plane(z):
            for ref, start in zip(refs, pieces):
                if start <= z < start + ref.shape[0]:
                    return [ref[z - start, f, :, lanes] for f in range(6)]

        state = plane(-HALF)
        for z in range(-HALF + 1, 1):
            state = [DECAY * s + v for s, v in zip(state, plane(z))]
        for f in range(6):
            part[0, f] = state[f]
        for z in range(1, planes):
            new, old = plane(z), plane(z - HALF - 1)
            state = [DECAY * s + (v - CUT * w) for s, v, w in zip(state, new, old)]
            for f in range(6):
                part[z, f] = state[f]
        state = [DECAY * v for v in plane(planes + HALF - 1)]
        for z in range(planes + HALF - 2, planes - 1, -1):
            state = [DECAY * (s + v) for s, v in zip(state, plane(z))]
        for z in range(planes - 1, -1, -1):
            xx, yy, zz, xy, xz, yz = [part[z, f] + state[f] for f in range(6)]
            scale = -1.0 / (zz + EPSILON)
            inline[z, :, lanes] = xz * scale
            cross[z, :, lanes] = yz * scale
            trace = xx + yy + zz
            minors = xx * yy + xx * zz + yy * zz - xy * xy - xz * xz - yz * yz
            coherent[z, :, lanes] = 1.0 - 3.0 * minors / (trace * trace + EPSILON)
            if z:
                near, far_plane = plane(z), plane(z + HALF)
                state = [DECAY * (s + v) - CUT * w for s, v, w in zip(state, near, far_plane)]


def send(x, axis, target):
    devices = lax.axis_size(axis)
    pairs = [(i, target(i)) for i in range(devices) if 0 <= target(i) < devices]
    return lax.ppermute(x, axis, pairs)


def local(volume):
    planes, rows, width = volume.shape
    groups = lax.axis_size("pa")
    device = lax.axis_index("pa")
    depth = lax.rem(lax.axis_index("gz"), 2)
    turn = lax.rem(device, 2) == lax.rem(device // 2, 2)
    halo = 8

    def cross(x):
        return send(x, "pa", lambda i: i ^ 1)

    def near(x):
        return send(x, "pa", lambda i: i ^ 2)

    def away(x):
        return send(x, "pa", lambda i: i - 2 if i % 4 < 2 else i + 2)

    def depth_near(x):
        return send(x, "gz", lambda i: i ^ 1)

    def depth_away(x):
        return send(x, "gz", lambda i: i - 1 if i % 2 == 0 else i + 1)

    def ordered(one, two):
        return jnp.where(low, two, one), jnp.where(low, one, two)

    low = lax.rem(device // 2, 2) == 0
    own = volume.transpose(1, 0, 2)
    near_own, away_own, other = near(own), away(own), cross(own)
    near_far, away_far = near(away_own), away(near_own)
    near_other, away_other = near(other), away(other)
    last_far = cross(jnp.where(turn, near_far, away_far))
    pieces = [own, *ordered(near_own, away_own), other, *ordered(near_far, away_far)]
    pieces += [*ordered(near_other, away_other), last_far]
    def end_planes(blocks, first):
        upper = jnp.concatenate([x[:, :halo] for x in blocks], axis=0)
        lower = jnp.concatenate([x[:, planes - halo :] for x in blocks], axis=0)
        return jnp.where(first, upper, lower)

    even = depth == 0
    swap_away = [depth_away(end_planes(x, even)) for x in (pieces[:4], pieces[4:])]
    swap_near = [depth_near(end_planes(pieces, jnp.logical_not(even)))]

    weights = []
    for matrix in (
        inline_matrix(SLOPE, width), inline_matrix(SMOOTH, width), average_matrix(width)
    ):
        weights += [jnp.asarray(w) for w in split_constant(matrix)]
    matrix = np.concatenate(split_constant(tile_matrix(8, 8)), axis=0)
    weights = [jnp.asarray(matrix)] + weights
    outer = rows + 2 * HALF

    def tensors(tiles, halos, kind, name):
        used = 8 * len(tiles)
        operands = pieces + halos + weights
        return pl.pallas_call(
            functools.partial(
                tensor_kernel, rows, rows * groups, tiles, width, kind
            ),
            out_shape=jax.ShapeDtypeStruct((used, 6, rows, width), F32),
            in_specs=[whole] * len(operands),
            out_specs=whole,
            scratch_shapes=[
                pltpu.VMEM((len(tiles), 9 * rows * 24, width), BF16),
                pltpu.VMEM((len(tiles), 9 * rows * 24, width), BF16),
                pltpu.VMEM((3, outer * used, width), BF16),
                pltpu.VMEM((3, outer * used, width), BF16),
                pltpu.VMEM((3, outer * used, width), F32),
                pltpu.VMEM((6, rows, 8, 128), F32),
                pltpu.VMEM((width // 128, 6, used * rows, 128), F32),
            ],
            compiler_params=pltpu.CompilerParams(vmem_limit_bytes=28 * 2**20),
            cost_estimate=pl.CostEstimate(
                flops=8 * 10**9, bytes_accessed=4 * 2**20, transcendentals=0
            ),
            name=name,
        )(*operands)

    whole = pl.BlockSpec(memory_space=pltpu.VMEM)
    middle = tensors([8, 16], [], None, "tensor_middle")
    middle_away = depth_away(middle)
    middle_near = depth_near(middle)
    end_away = tensors([0], swap_away, (2, "away"), "tensor_away")
    from_away = depth_away(end_away)
    end_near = tensors([0], swap_near, (1, "near"), "tensor_near")
    from_near = depth_near(end_near)
    arrays = [middle, end_near, end_away, from_near, middle_near, from_away, middle_away]
    starts = [-HALF, -halo, 0, halo, planes - halo, planes, planes + halo]
    shape = jax.ShapeDtypeStruct((planes, rows, width), F32)
    return tuple(
        pl.pallas_call(
            functools.partial(attribute_kernel, planes, width, starts),
            out_shape=[shape] * 3,
            in_specs=[whole] * len(arrays),
            out_specs=[whole] * 3,
            scratch_shapes=[pltpu.VMEM((planes, 6, 8, 128), F32)],
            compiler_params=pltpu.CompilerParams(vmem_limit_bytes=28 * 2**20),
            name="attributes",
        )(*arrays)
    )


def solution(mesh):
    placed = P("gz", "pa", None)
    return jax.shard_map(
        local,
        mesh=mesh,
        in_specs=(placed,),
        out_specs=(placed, placed, placed),
        check_vma=False,
    )
```

```python
import functools
import math

import jax
import jax.numpy as jnp
import numpy as np
from jax import lax
from jax.experimental import pallas as pl
from jax.experimental.pallas import tpu as pltpu
from jax.sharding import PartitionSpec as P

HALF = 24
GHALF = 6
SIGMA_GRADIENT = 1.5
DECAY_LENGTH = 4.0
EPSILON = 1e-06

REACH = HALF + GHALF
DECAY = math.exp(-1.0 / DECAY_LENGTH)
CUT = math.exp(-(HALF + 1) / DECAY_LENGTH)
BF16 = jnp.bfloat16
F32 = jnp.float32


def gradient_taps():
    k = np.arange(-GHALF, GHALF + 1).astype(np.float64)
    bell = np.exp(-k * k / (2.0 * SIGMA_GRADIENT**2))
    smooth = bell / np.sqrt(np.sum(bell * bell))
    slope = k * bell / np.sqrt(np.sum((k * bell) ** 2))
    return smooth, slope


def average_scale():
    k = np.arange(-HALF, HALF + 1).astype(np.float64)
    return 1.0 / np.sum(np.exp(-np.abs(k) / DECAY_LENGTH))


SMOOTH, SLOPE = gradient_taps()


def split_constant(matrix):
    matrix = matrix.astype(np.float32)
    high = matrix.astype(BF16)
    low = (matrix - high.astype(np.float32)).astype(BF16)
    return high, low


def inline_matrix(taps, length):
    reach = (len(taps) - 1) // 2
    offset = np.arange(length)[:, None] - np.arange(length)[None, :]
    inside = np.abs(offset) <= reach
    return np.where(inside, taps[np.clip(offset + reach, 0, 2 * reach)], 0.0)


def average_matrix(length):
    offset = np.abs(np.arange(length)[:, None] - np.arange(length)[None, :])
    values = np.exp(-offset / DECAY_LENGTH) * average_scale() ** 3
    return np.where(offset <= HALF, values, 0.0)


def tile_matrix(rows, planes):
    def band(taps, outputs, inputs, lead):
        offset = np.arange(inputs)[None, :] - np.arange(outputs)[:, None] - lead
        inside = np.abs(offset) <= GHALF
        return np.where(inside, taps[np.clip(offset + GHALF, 0, 2 * GHALF)], 0.0)

    def pair(cross, depth):
        cross = band(cross, rows, rows + 2 * GHALF, GHALF)
        depth = band(depth, planes, 3 * planes, planes)
        return np.kron(cross, depth)

    return np.concatenate(
        [pair(SMOOTH, SMOOTH), pair(SLOPE, SMOOTH), pair(SMOOTH, SLOPE)], axis=0
    )


def split(x):
    high = x.astype(BF16)
    low = (x - high.astype(F32)).astype(BF16)
    return high, low


def dot(a, b):
    return jnp.dot(a, b, preferred_element_type=F32)


def dot3(x, w_high, w_low):
    high, low = split(x)
    return dot(high, w_high) + (dot(high, w_low) + dot(low, w_high))


def gradient_rows(tile_count, groups, first_row, total_rows, trim, weights, raw, pre, write):
    taps, wd_high, wd_low, wg_high, wg_low = weights
    (raw_high, raw_low), (pre_high, pre_low) = raw, pre
    group, width = 8, raw_high.shape[2]
    size = group * 8
    reach = (group + 2 * GHALF) * 24
    for n in range(tile_count):
        for g in range(groups):
            at = (g * group + trim) * 24
            high, low = raw_high[n, at : at + reach, :], raw_low[n, at : at + reach, :]
            both = dot(taps[...], high)
            result = both[: 3 * size] + (both[3 * size :] + dot(taps[: 3 * size, :], low))
            row = first_row + g * group + lax.broadcasted_iota(jnp.int32, (size, width), 0) // 8
            inside = jnp.logical_and(row >= 0, row < total_rows).astype(F32)
            to = (n * groups + g) * size
            for f in range(3):
                high, low = split(result[f * size : (f + 1) * size] * inside)
                pre_high[f, to : to + size, :] = high
                pre_low[f, to : to + size, :] = low
    for f, (w_high, w_low) in enumerate(
        ((wd_high, wd_low), (wg_high, wg_low), (wg_high, wg_low))
    ):
        for n in range(tile_count):
            at = slice(n * groups * size, (n + 1) * groups * size)
            high, low = pre_high[f, at, :], pre_low[f, at, :]
            write(f, n, dot(high, w_high[...]) + (dot(high, w_low[...]) + dot(low, w_high[...])))


def stage_rows(raw, n, place, x):
    rows, width = x.shape[0] * x.shape[1], x.shape[2]
    high, low = split(x.reshape(rows, width))
    at = pl.ds(pl.multiple_of(place * rows, 16), rows)
    raw[0][n, at, :] = high
    raw[1][n, at, :] = low


def stage_window(raw, tiles, blocks, even_order, odd_order):
    def stage(order):
        for n, plane in enumerate(tiles):
            for place, index in enumerate(order):
                stage_rows(raw, n, place, blocks[index][:, plane - 8 : plane + 16])

    odd = lax.rem(lax.axis_index("pa"), 2) == 1
    pl.when(odd)(lambda: stage(odd_order))
    pl.when(jnp.logical_not(odd))(lambda: stage(even_order))


def early_kernel(rows, total_rows, tiles, *refs):
    blocks, weights, out = refs[:8], refs[8:13], refs[13]
    raw, pre = refs[14:16], refs[16:18]
    device = lax.axis_index("pa")
    even = 1 - lax.rem(device, 2)
    stage_window(raw, tiles, blocks, (1, 6, 0, 3, 2, 7, 5), (4, 6, 1, 3, 0, 7, 2))

    def write(f, n, result):
        out[f, n] = result

    gradient_rows(
        len(tiles), 5, device * rows - HALF + 16 * even, total_rows, 4 * rows - REACH,
        weights, raw, pre, write,
    )


def tensor_kernel(rows, total_rows, tiles, width, halos, *refs):
    blocks, refs = refs[:9], refs[9:]
    count, upper_side = halos
    halo, refs = refs[:count], refs[count:]
    weights, ws_high, ws_low, out = refs[:5], refs[5], refs[6], refs[7]
    raw_high, raw_low, pre_high, pre_low, grads, part, ty = refs[-7:]
    raw, pre = (raw_high, raw_low), (pre_high, pre_low)
    tile_count = len(tiles)
    planes = 8 * tile_count
    device = lax.axis_index("pa")
    odd = lax.rem(device, 2)
    side = 1 - 2 * odd
    even_depth = lax.rem(lax.axis_index("gz"), 2) == 0
    outer = rows + 2 * HALF
    trim = 4 * rows - REACH
    places = [0, -2, 2, side, -4, 4, side - 2, side + 2, -3 * side]

    def stage_end(first):
        for i, (block, place) in enumerate(zip(blocks, places)):
            part, at = (halo[0], i) if i < 4 or count == 1 else (halo[1], i - 4)
            beyond = part[at * rows : (at + 1) * rows]
            parts = [beyond, block[:, :16]] if first else [block[:, -16:], beyond]
            stage_rows(raw, 0, place + 4, jnp.concatenate(parts, axis=1))

    first_row = device * rows - HALF
    if upper_side == "middle":
        early = halo[0]
        stage_window(raw, tiles, blocks, (4, 8, 1, 6), (7, 2, 8, 5))
        for f in range(3):
            for n in range(tile_count):
                at = pl.multiple_of(n * outer * 8 + (1 - odd) * 128, 8)
                grads[f, pl.ds(at, 320), :] = early[f, n]

        def write(f, n, result):
            grads[f, pl.ds(pl.multiple_of(n * outer * 8 + odd * 320, 8), 128), :] = result

        gradient_rows(
            tile_count, 2, first_row + 40 * odd, total_rows, trim, weights, raw, pre, write
        )
    else:
        upper = even_depth if upper_side == "away" else jnp.logical_not(even_depth)
        pl.when(upper)(lambda: stage_end(True))
        pl.when(jnp.logical_not(upper))(lambda: stage_end(False))

        def write(f, n, result):
            grads[f, n * outer * 8 : (n + 1) * outer * 8, :] = result

        gradient_rows(tile_count, 7, first_row, total_rows, trim, weights, raw, pre, write)

    def products(j, at, lanes):
        x, y, z = (grads[f, pl.ds(at + 8 * j, 8), lanes] for f in range(3))
        return [x * x, y * y, z * z, x * y, x * z, y * z]

    for lane in range(0, width, 128):
        lanes = slice(lane, lane + 128)

        def average_rows(t, carry, lane=lane, lanes=lanes):
            at = pl.multiple_of(t * (outer * 8), 8)
            state = products(0, at, lanes)
            for j in range(1, HALF + 1):
                state = [DECAY * s + v for s, v in zip(state, products(j, at, lanes))]
            for f in range(6):
                part[f, 0] = state[f]
            for i in range(1, rows):
                new, old = products(HALF + i, at, lanes), products(i - 1, at, lanes)
                state = [DECAY * s + (v - CUT * w) for s, v, w in zip(state, new, old)]
                for f in range(6):
                    part[f, i] = state[f]
            state = [DECAY * v for v in products(outer - 1, at, lanes)]
            for j in range(outer - 2, HALF + rows - 1, -1):
                state = [DECAY * (s + v) for s, v in zip(state, products(j, at, lanes))]
            for i in range(rows - 1, -1, -1):
                for f in range(6):
                    ty[lane // 128, f, pl.ds(t * 8 * rows + i, 8, stride=rows), :] = part[f, i] + state[f]
                if i:
                    near, far_row = products(HALF + i, at, lanes), products(2 * HALF + i, at, lanes)
                    state = [
                        DECAY * (s + v) - CUT * w for s, v, w in zip(state, near, far_row)
                    ]
            return carry

        lax.fori_loop(0, tile_count, average_rows, 0)

    for f in range(6):
        held = jnp.concatenate([ty[h, f] for h in range(width // 128)], axis=1)
        field = dot3(held, ws_high[...], ws_low[...]).reshape(planes, rows, width)
        out[:, f] = field


def attribute_kernel(planes, width, pieces, *refs):
    inline, cross, coherent, part = refs[-4:]
    middle, end_near, end_away, ends_a, middle_a, ends_b, middle_b = refs[:7]
    even_depth = lax.rem(lax.axis_index("gz"), 2) == 0
    results = (inline, cross, coherent, part)
    pl.when(even_depth)(
        lambda: attributes(
            planes, width, pieces,
            (middle_b, ends_b, end_away, middle, end_near, ends_a, middle_a), *results
        )
    )
    pl.when(jnp.logical_not(even_depth))(
        lambda: attributes(
            planes, width, pieces,
            (middle_a, ends_a, end_near, middle, end_away, ends_b, middle_b), *results
        )
    )


def attributes(planes, width, pieces, refs, inline, cross, coherent, part):
    for lane in range(0, width, 128):
        lanes = slice(lane, lane + 128)

        def plane(z):
            for ref, start in zip(refs, pieces):
                if start <= z < start + ref.shape[0]:
                    return [ref[z - start, f, :, lanes] for f in range(6)]

        state = plane(-HALF)
        for z in range(-HALF + 1, 1):
            state = [DECAY * s + v for s, v in zip(state, plane(z))]
        for f in range(6):
            part[0, f] = state[f]
        for z in range(1, planes):
            new, old = plane(z), plane(z - HALF - 1)
            state = [DECAY * s + (v - CUT * w) for s, v, w in zip(state, new, old)]
            for f in range(6):
                part[z, f] = state[f]
        state = [DECAY * v for v in plane(planes + HALF - 1)]
        for z in range(planes + HALF - 2, planes - 1, -1):
            state = [DECAY * (s + v) for s, v in zip(state, plane(z))]
        for z in range(planes - 1, -1, -1):
            xx, yy, zz, xy, xz, yz = [part[z, f] + state[f] for f in range(6)]
            scale = -1.0 / (zz + EPSILON)
            inline[z, :, lanes] = xz * scale
            cross[z, :, lanes] = yz * scale
            trace = xx + yy + zz
            minors = xx * yy + xx * zz + yy * zz - xy * xy - xz * xz - yz * yz
            coherent[z, :, lanes] = 1.0 - 3.0 * minors / (trace * trace + EPSILON)
            if z:
                near, far_plane = plane(z), plane(z + HALF)
                state = [DECAY * (s + v) - CUT * w for s, v, w in zip(state, near, far_plane)]


def send(x, axis, target):
    devices = lax.axis_size(axis)
    pairs = [(i, target(i)) for i in range(devices) if 0 <= target(i) < devices]
    return lax.ppermute(x, axis, pairs)


def local(volume):
    planes, rows, width = volume.shape
    groups = lax.axis_size("pa")
    device = lax.axis_index("pa")
    depth = lax.rem(lax.axis_index("gz"), 2)
    turn = lax.rem(device, 2) == lax.rem(device // 2, 2)
    halo = 8

    def cross(x):
        return send(x, "pa", lambda i: i ^ 1)

    def near(x):
        return send(x, "pa", lambda i: i ^ 2)

    def away(x):
        return send(x, "pa", lambda i: i - 2 if i % 4 < 2 else i + 2)

    def depth_near(x):
        return send(x, "gz", lambda i: i ^ 1)

    def depth_away(x):
        return send(x, "gz", lambda i: i - 1 if i % 2 == 0 else i + 1)

    def ordered(one, two):
        return jnp.where(low, two, one), jnp.where(low, one, two)

    low = lax.rem(device // 2, 2) == 0
    own = volume.transpose(1, 0, 2)
    near_own, away_own, other = near(own), away(own), cross(own)
    near_far, away_far = near(away_own), away(near_own)
    near_other, away_other = near(other), away(other)
    last_far = cross(jnp.where(turn, near_far, away_far))
    pieces = [own, *ordered(near_own, away_own), other, *ordered(near_far, away_far)]
    pieces += [*ordered(near_other, away_other), last_far]
    def end_planes(blocks, first):
        upper = jnp.concatenate([x[:, :halo] for x in blocks], axis=0)
        lower = jnp.concatenate([x[:, planes - halo :] for x in blocks], axis=0)
        return jnp.where(first, upper, lower)

    even = depth == 0
    swap_away = [depth_away(end_planes(x, even)) for x in (pieces[:4], pieces[4:])]
    swap_near = [depth_near(end_planes(pieces, jnp.logical_not(even)))]

    weights = []
    for matrix in (
        inline_matrix(SLOPE, width), inline_matrix(SMOOTH, width), average_matrix(width)
    ):
        weights += [jnp.asarray(w) for w in split_constant(matrix)]
    matrix = np.concatenate(split_constant(tile_matrix(8, 8)), axis=0)
    weights = [jnp.asarray(matrix)] + weights
    outer = rows + 2 * HALF

    def tensors(tiles, halos, kind, name):
        used = 8 * len(tiles)
        operands = pieces + halos + weights
        return pl.pallas_call(
            functools.partial(
                tensor_kernel, rows, rows * groups, tiles, width, kind
            ),
            out_shape=jax.ShapeDtypeStruct((used, 6, rows, width), F32),
            in_specs=[whole] * len(operands),
            out_specs=whole,
            scratch_shapes=[
                pltpu.VMEM((len(tiles), 9 * rows * 24, width), BF16),
                pltpu.VMEM((len(tiles), 9 * rows * 24, width), BF16),
                pltpu.VMEM((3, outer * used, width), BF16),
                pltpu.VMEM((3, outer * used, width), BF16),
                pltpu.VMEM((3, outer * used, width), F32),
                pltpu.VMEM((6, rows, 8, 128), F32),
                pltpu.VMEM((width // 128, 6, used * rows, 128), F32),
            ],
            compiler_params=pltpu.CompilerParams(vmem_limit_bytes=28 * 2**20),
            cost_estimate=pl.CostEstimate(
                flops=8 * 10**9, bytes_accessed=4 * 2**20, transcendentals=0
            ),
            name=name,
        )(*operands)

    whole = pl.BlockSpec(memory_space=pltpu.VMEM)
    tiles = [8, 16]
    early_shape = (len(tiles), 7 * rows * 24, width)
    early_pre = (3, len(tiles) * 320, width)
    early = pl.pallas_call(
        functools.partial(early_kernel, rows, rows * groups, tiles),
        out_shape=jax.ShapeDtypeStruct((3, len(tiles), 320, width), F32),
        in_specs=[whole] * 13,
        out_specs=whole,
        scratch_shapes=[pltpu.VMEM(early_shape, BF16)] * 2 + [pltpu.VMEM(early_pre, BF16)] * 2,
        compiler_params=pltpu.CompilerParams(vmem_limit_bytes=28 * 2**20),
        cost_estimate=pl.CostEstimate(
            flops=4 * 10**9, bytes_accessed=4 * 2**20, transcendentals=0
        ),
        name="early",
    )(*pieces[:8], *weights[:5])
    middle = tensors(tiles, [early], (1, "middle"), "tensor_middle")
    middle_away = depth_away(middle)
    middle_near = depth_near(middle)
    end_away = tensors([0], swap_away, (2, "away"), "tensor_away")
    from_away = depth_away(end_away)
    end_near = tensors([0], swap_near, (1, "near"), "tensor_near")
    from_near = depth_near(end_near)
    arrays = [middle, end_near, end_away, from_near, middle_near, from_away, middle_away]
    starts = [-HALF, -halo, 0, halo, planes - halo, planes, planes + halo]
    shape = jax.ShapeDtypeStruct((planes, rows, width), F32)
    return tuple(
        pl.pallas_call(
            functools.partial(attribute_kernel, planes, width, starts),
            out_shape=[shape] * 3,
            in_specs=[whole] * len(arrays),
            out_specs=[whole] * 3,
            scratch_shapes=[pltpu.VMEM((planes, 6, 8, 128), F32)],
            compiler_params=pltpu.CompilerParams(vmem_limit_bytes=28 * 2**20),
            name="attributes",
        )(*arrays)
    )


def solution(mesh):
    placed = P("gz", "pa", None)
    return jax.shard_map(
        local,
        mesh=mesh,
        in_specs=(placed,),
        out_specs=(placed, placed, placed),
        check_vma=False,
    )
```
